128 devices in a mesh: polar: 16 (over x_hi, y, core), azimuth: 8 (over x_lo, z).
Axes of the slice: x: 4 (x_hi: 2, x_lo: 2; x = x_hi * 2 + x_lo), y: 4, z: 4, core: 2. Of those that a mesh axis runs over, the one named last changes fastest.
Arguments:
- grid_input: bfloat16 [720, 276480], P('polar', 'azimuth'), may hold values from -6 to 6
- cotangent: bfloat16 [720, 192, 1440], P('polar', 'azimuth'), may hold values from -6 to 6
- forward_legendre: bfloat16 [720, 256, 256], P(None, 'polar'), may hold values from -0.21875 to 0.21875
- inverse_legendre: bfloat16 [720, 256, 256], P(None, 'polar'), may hold values from -0.375 to 0.375
- filter_weight: bfloat16 [256, 73728], P('polar'), may hold values from -0.3125 to 0.3125
Outputs:
- filtered: bfloat16 [720, 192, 1440], P('polar', 'azimuth')
- grid_grad: bfloat16 [720, 276480], P('polar', 'azimuth')
The draws below stay inside these ranges and needn't reach their ends.
All inputs are finite; a program needn't handle non-finite values.
Results may differ from the reference program's by a relative error of at most 0.02.
Values may be sent and summed in bfloat16 or wider, within the bound.
No kernel may reach another device: no remote copies, remote signals or barrier semaphores. Data moves between devices by JAX's collectives and lax.ppermute only.
A program may use at most 256 MiB of HBM per device.

```python
import math
import jax
import jax.numpy as jnp
from jax import lax

LAT = 720
LON = 1440
C = 192
DEGREES = 256
ORDERS = 256
N_POLAR = 16


def level_of(rng, extent, pieces, low, largest):
    def one(position, blocks):
        draws = jax.random.uniform(jax.random.fold_in(jax.random.fold_in(rng, 6), position), (blocks,), jnp.float32, low / len(pieces), largest / len(pieces))
        return jnp.repeat(jnp.exp(draws), extent[position] // blocks).reshape((-1,) + (1,) * (len(extent) - position - 1))

    level = one(*pieces[0])
    for cut in pieces[1:]:
        level = level * one(*cut)
    return level


def normal_values(stream_key, dims, scale, bound, pieces=(), held_as=jnp.bfloat16):
    drawn = scale * jax.random.normal(stream_key, dims, jnp.float32)
    if pieces:
        drawn = drawn * level_of(stream_key, dims, pieces, -0.22, 0.18)
    return jnp.clip(drawn, -bound, bound).astype(held_as)


def setup_inputs(seed: int = 0) -> dict:
    arg_keys = jax.random.split(jax.random.key(seed), 6)
    grid_input = normal_values(arg_keys[0], (LAT, LON * C), 1.0, 6.0, ((0, 16), (1, 8)))
    cotangent = normal_values(arg_keys[1], (LAT, C, LON), 1.0, 6.0, ((0, 16), (1, 8)))
    forward_legendre = normal_values(arg_keys[2], (LAT, ORDERS, DEGREES), LAT ** -0.5, 0.21875, ((1, 16),))
    inverse_legendre = normal_values(arg_keys[3], (LAT, ORDERS, DEGREES), DEGREES ** -0.5, 0.375, ((1, 16),))
    filter_weight = normal_values(arg_keys[4], (DEGREES, 2 * C * C), (2 * C) ** -0.5, 0.3125, ((0, 16),))
    return {"grid_input": grid_input, "cotangent": cotangent, "forward_legendre": forward_legendre, "inverse_legendre": inverse_legendre, "filter_weight": filter_weight}


def make_tables():
    longitude = jnp.arange(LON, dtype=jnp.int32)
    order_index = jnp.arange(ORDERS, dtype=jnp.int32)
    phases = (longitude[:, None] * order_index[None, :] % LON).astype(jnp.float32)
    angles = phases * (2.0 * math.pi / LON)
    factor = 1.0 / math.sqrt(LON)
    stacked = jnp.stack([jnp.cos(angles) * factor, -jnp.sin(angles) * factor], axis=-1)
    doubling = jnp.where(order_index == 0, 1.0, 2.0).astype(jnp.float32)
    basis_plain = stacked.reshape(LON, 2 * ORDERS).astype(jnp.bfloat16)
    basis_doubled = (stacked * doubling[None, :, None]).reshape(LON, 2 * ORDERS).astype(jnp.bfloat16)
    return (basis_plain, basis_doubled)

def degree_sum(field, matrix):
    row_count = LAT // N_POLAR
    running = jnp.zeros((DEGREES, ORDERS, 2, C), jnp.float32)
    for block in range(N_POLAR):
        field_part = field[block * row_count:(block + 1) * row_count].astype(jnp.float32)
        matrix_part = matrix[block * row_count:(block + 1) * row_count].astype(jnp.float32)
        partial_sum = jnp.einsum('amrc,aml->lmrc', field_part, matrix_part)
        rounded = lax.optimization_barrier(partial_sum.astype(jnp.bfloat16))
        running = running + rounded.astype(jnp.float32)
    return running.astype(jnp.bfloat16)

def degree_rows(modes, matrix):
    return jnp.einsum('lmrc,aml->amrc', modes.astype(jnp.float32), matrix.astype(jnp.float32)).astype(jnp.bfloat16)

def reference(grid_input, cotangent, forward_legendre, inverse_legendre, filter_weight):
    basis_plain, basis_doubled = make_tables()
    plain_wide = basis_plain.astype(jnp.float32)
    doubled_wide = basis_doubled.astype(jnp.float32)
    grid_cube = grid_input.reshape(LAT, LON, C)
    spectrum = jnp.einsum('alc,lj->ajc', grid_cube.astype(jnp.float32), plain_wide)
    spectrum = spectrum.astype(jnp.bfloat16).reshape(LAT, ORDERS, 2, C)
    coefficients = degree_sum(spectrum, forward_legendre).astype(jnp.float32)
    weight_cube = filter_weight.reshape(DEGREES, 2, C, C)
    weight_real = weight_cube[:, 0].astype(jnp.float32)
    weight_imag = weight_cube[:, 1].astype(jnp.float32)
    mixed_real = jnp.einsum('lmc,lco->lmo', coefficients[:, :, 0], weight_real) - jnp.einsum('lmc,lco->lmo', coefficients[:, :, 1], weight_imag)
    mixed_imag = jnp.einsum('lmc,lco->lmo', coefficients[:, :, 0], weight_imag) + jnp.einsum('lmc,lco->lmo', coefficients[:, :, 1], weight_real)
    mixed_modes = jnp.stack([mixed_real, mixed_imag], axis=2).astype(jnp.bfloat16)
    synthesis = degree_rows(mixed_modes, inverse_legendre)
    filtered = jnp.einsum('ajc,lj->acl', synthesis.reshape(LAT, 2 * ORDERS, C).astype(jnp.float32), doubled_wide).astype(jnp.bfloat16)
    grad_synthesis = jnp.einsum('acl,lj->ajc', cotangent.astype(jnp.float32), doubled_wide)
    grad_synthesis = grad_synthesis.astype(jnp.bfloat16).reshape(LAT, ORDERS, 2, C)
    grad_mixed = degree_sum(grad_synthesis, inverse_legendre).astype(jnp.float32)
    grad_real = jnp.einsum('lmo,lco->lmc', grad_mixed[:, :, 0], weight_real) + jnp.einsum('lmo,lco->lmc', grad_mixed[:, :, 1], weight_imag)
    grad_imag = jnp.einsum('lmo,lco->lmc', grad_mixed[:, :, 1], weight_real) - jnp.einsum('lmo,lco->lmc', grad_mixed[:, :, 0], weight_imag)
    grad_coefficients = jnp.stack([grad_real, grad_imag], axis=2).astype(jnp.bfloat16)
    grad_spectrum = degree_rows(grad_coefficients, forward_legendre)
    grid_grad = jnp.einsum('ajc,lj->alc', grad_spectrum.reshape(LAT, 2 * ORDERS, C).astype(jnp.float32), plain_wide).astype(jnp.bfloat16)
    return (filtered, grid_grad.reshape(LAT, LON * C))
```

```python
import functools
import math
import numpy as np
import ml_dtypes
import jax
import jax.numpy as jnp
from jax import lax
from jax.sharding import PartitionSpec as P
from jax.experimental import pallas as pl
from jax.experimental.pallas import tpu as pltpu

LAT = 720
LON = 1440
C = 192
DEG = 256
ORD = 256
NP = 16
NA = 8
ROWS = 45
SLOTS = 6
PAIRS = 90
LP = 96
W = 1152
F32 = jnp.float32
BF = jnp.bfloat16


def params():
    return pltpu.CompilerParams(vmem_limit_bytes=56 << 20)


def dot(a, b, ca, cb):
    return lax.dot_general(a, b, (((ca,), (cb,)), ((), ())), preferred_element_type=F32)


def tables():
    lon = np.arange(LON)[:, None]
    m = np.arange(ORD)[None, :]
    ang = ((lon * m) % LON) * (2.0 * math.pi / LON)
    fac = 1.0 / math.sqrt(LON)
    st = np.stack([np.cos(ang) * fac, -np.sin(ang) * fac], axis=-1).astype(np.float32)
    dbl = np.where(np.arange(ORD) == 0, 1.0, 2.0).astype(np.float32)[None, :, None]
    plain = st.reshape(LON, 2 * ORD).astype(ml_dtypes.bfloat16)
    doubled = (st * dbl).reshape(LON, 2 * ORD).astype(ml_dtypes.bfloat16)
    p4 = plain.reshape(NA, PAIRS, 2, 2 * ORD).transpose(2, 0, 1, 3)
    pp = np.zeros((2, NA, LP, 2 * ORD), ml_dtypes.bfloat16)
    pp[:, :, :PAIRS] = p4
    pp = pp.reshape(2 * NA * LP, 2 * ORD)
    return np.ascontiguousarray(doubled.T), np.ascontiguousarray(pp.T), pp


def prep_body(x_ref, o_ref, s_ref):
    step = pl.program_id(0)
    lane = lax.broadcasted_iota(jnp.int32, (8, 6144), 1) + step * 6144
    good = lane < PAIRS * 384
    for k in range(SLOTS):
        if k < 5:
            v = x_ref[8 * k:8 * k + 8, :].astype(F32)
        else:
            v = jnp.concatenate([x_ref[40:45, :].astype(F32), jnp.zeros((3, 6144), F32)], 0)
        v = jnp.where(good, v, 0.0)
        for lp in range(16):
            for t in range(3):
                s_ref[3 * k + t, pl.ds(lp, 8, stride=16), :] = v[:, (3 * lp + t) * 128:(3 * lp + t + 1) * 128]
    for a in range(NA):
        for q in range(18):
            o_ref[a, :, q * 128:(q + 1) * 128] = s_ref[q, 16 * a:16 * a + 16, :].astype(BF)


def prep(x):
    return pl.pallas_call(
        prep_body,
        grid=(6,),
        out_shape=jax.ShapeDtypeStruct((NA, LP, 2304), BF),
        in_specs=[pl.BlockSpec((ROWS, 6144), lambda i: (0, i))],
        out_specs=pl.BlockSpec((NA, 16, 2304), lambda i: (0, i, 0)),
        scratch_shapes=[pltpu.VMEM((18, 128, 128), F32)],
        compiler_params=params(),
        name="prep",
    )(x)


def post_body(r_ref, o_ref, s_ref):
    for a in range(NA):
        for q in range(18):
            s_ref[q, 16 * a:16 * a + 16, :] = r_ref[a, :, q * 128:(q + 1) * 128].astype(F32)
    for k in range(SLOTS):
        for lp in range(16):
            for t in range(3):
                v = s_ref[3 * k + t, pl.ds(lp, 8, stride=16), :].astype(BF)
                n = 8 if k < 5 else 5
                o_ref[8 * k:8 * k + n, (3 * lp + t) * 128:(3 * lp + t + 1) * 128] = v[:n]


def post(r):
    return pl.pallas_call(
        post_body,
        grid=(6,),
        out_shape=jax.ShapeDtypeStruct((ROWS, LON // NA * C), BF),
        in_specs=[pl.BlockSpec((NA, 16, 2304), lambda i: (0, i, 0))],
        out_specs=pl.BlockSpec((ROWS, 6144), lambda i: (0, i)),
        scratch_shapes=[pltpu.VMEM((18, 128, 128), F32)],
        compiler_params=params(),
        name="post",
    )(r)


def whole(body, out, *args, scratch=(), name=None):
    return pl.pallas_call(
        body,
        out_shape=jax.ShapeDtypeStruct(out, BF),
        scratch_shapes=list(scratch),
        compiler_params=params(),
        name=name,
    )(*args)


def dft_f_body(r_ref, b_ref, o_ref, x_ref):
    for k in range(SLOTS):
        v = r_ref[:, :, 384 * k:384 * k + 384].reshape(NA * LP, 384)
        x_ref[0:768, C * k:C * k + C] = v[:, :C]
        x_ref[768:1536, C * k:C * k + C] = v[:, C:]
    y = dot(b_ref[...], x_ref[...], 1, 0).astype(BF)
    o_ref[...] = y.reshape(128, 4, W)


def dft_f(r, bpt):
    return whole(dft_f_body, (128, 4, W), r, bpt, scratch=[pltpu.VMEM((1536, W), BF)], name="dft_f")


def dft_g_body(x_ref, b_ref, o_ref):
    y = dot(b_ref[...], x_ref[...], 1, 1).astype(BF)
    y = jnp.concatenate([y, jnp.zeros((512, W - 1080), BF)], 1)
    o_ref[...] = y.reshape(128, 4, W)


def dft_g(x, bdt):
    return whole(dft_g_body, (128, 4, W), x, bdt, name="dft_g")


def leg_f_body(r_ref, p_ref, o_ref, s_ref):
    for m in range(2):
        for r in range(2):
            v = r_ref[:, 2 * m + r, :]
            for k in range(SLOTS):
                s_ref[128 * k:128 * k + 128, C * r:C * r + C] = v[:, C * k:C * k + C]
        y = dot(p_ref[m], s_ref[...], 0, 0).astype(BF)
        o_ref[:, 384 * m:384 * m + 384] = y


def leg_f(r, pf):
    return whole(leg_f_body, (DEG, 768), r, pf, scratch=[pltpu.VMEM((768, 384), BF)], name="leg_f")


def leg_g_body(r_ref, p_ref, o_ref, s_ref):
    for m in range(2):
        for r in range(2):
            v = r_ref[:, 2 * m + r, :].astype(F32).reshape(NP, NA, W)
            for a in range(NA):
                va = v[:, a, :].astype(BF)
                for t in range(48):
                    s_ref[16 * t:16 * t + 16, C * r + 24 * a:C * r + 24 * a + 24] = va[:, 24 * t:24 * t + 24]
        y = dot(p_ref[m], s_ref[...], 0, 0).astype(BF)
        o_ref[:, 384 * m:384 * m + 384] = y


def leg_g(r, pi):
    return whole(leg_g_body, (DEG, 768), r, pi, scratch=[pltpu.VMEM((768, 384), BF)], name="leg_g")


def mix_body(adjoint, r_ref, k_ref, o_ref, s_ref):
    i = lax.broadcasted_iota(jnp.int32, (256, 256), 0)
    j = lax.broadcasted_iota(jnp.int32, (256, 256), 1)
    perm = ((i // 16 == j % 16) & (i % 16 == j // 16)).astype(F32).astype(BF)
    x = dot(perm, r_ref[...].reshape(256, 768), 1, 0).astype(BF)
    for l in range(16):
        v = x[16 * l:16 * l + 16]
        v = jnp.concatenate([v[:, :384], v[:, 384:]], 0)
        y = dot(v, k_ref[l], 1, 1 if adjoint else 0).astype(BF)
        s_ref[16 * l:16 * l + 16, :384] = y[:16]
        s_ref[16 * l:16 * l + 16, 384:] = y[16:]
    o_ref[...] = dot(perm, s_ref[...], 1, 0).astype(BF).reshape(16, 16, 768)


def mix(r, k, adjoint):
    return whole(functools.partial(mix_body, adjoint), (16, 16, 768), r, k, scratch=[pltpu.VMEM((256, 768), BF)], name="mix_g" if adjoint else "mix_f")


def syn_f_body(x_ref, p_ref, o_ref, z_ref):
    for m in range(2):
        y = dot(p_ref[m], x_ref[:, 384 * m:384 * m + 384], 1, 0).astype(BF)
        for r in range(2):
            for a in range(NA):
                for t in range(48):
                    z_ref[a, :, 24 * t:24 * t + 24] = y[16 * t:16 * t + 16, C * r + 24 * a:C * r + 24 * a + 24]
            for p in range(NP):
                o_ref[8 * p:8 * p + 8, 2 * m + r, :] = z_ref[:, p, :]


def syn_f(x, pi):
    return whole(syn_f_body, (128, 4, W), x, pi, scratch=[pltpu.VMEM((8, 16, W), BF)], name="syn_f")


def syn_g_body(x_ref, p_ref, o_ref, z_ref):
    for m in range(2):
        y = dot(p_ref[m], x_ref[:, 384 * m:384 * m + 384], 1, 0).astype(BF)
        for r in range(2):
            for k in range(SLOTS):
                z_ref[:, C * k:C * k + C] = y[128 * k:128 * k + 128, C * r:C * r + C]
            o_ref[:, 2 * m + r, :] = z_ref[...]


def syn_g(x, pf):
    return whole(syn_g_body, (128, 4, W), x, pf, scratch=[pltpu.VMEM((128, W), BF)], name="syn_g")


def idft_f_body(y_ref, b_ref, o_ref):
    y = y_ref[...].reshape(512, W)
    o_ref[...] = dot(y[:, :1080], b_ref[...], 0, 0).astype(BF)


def idft_f(y, bdt):
    return whole(idft_f_body, (1080, LON), y, bdt, name="idft_f")


def idft_g_body(y_ref, b_ref, o_ref):
    y = y_ref[...].reshape(512, W)
    z = dot(b_ref[...], y, 1, 0).astype(BF)
    for k in range(SLOTS):
        e = z[:768, C * k:C * k + C].reshape(NA, LP, C)
        o = z[768:, C * k:C * k + C].reshape(NA, LP, C)
        o_ref[:, :, 384 * k:384 * k + 384] = jnp.concatenate([e, o], 2)


def idft_g(y, bp):
    return whole(idft_g_body, (NA, LP, 2304), y, bp, name="idft_g")


def order_tables(table, first):
    part = lax.dynamic_slice(table, (0, first, 0), (LAT, 2, DEG))
    part = part.reshape(NP, ROWS, 2, DEG).transpose(2, 0, 1, 3)
    return jnp.pad(part, ((0, 0), (0, 0), (0, 3), (0, 0)))


def on_device(grid_input, cotangent, forward_legendre, inverse_legendre, filter_weight):
    bdt, bpt, bp = [jnp.asarray(t) for t in tables()]
    both = ("polar", "azimuth")
    first = 2 * lax.axis_index("azimuth")
    wire_a = lax.all_to_all(prep(grid_input), "azimuth", 0, 0)

    wire_g = lax.all_to_all(dft_g(cotangent.reshape(1080, LON), bdt), both, 0, 0)

    pf = order_tables(forward_legendre, first)
    pf = pf.reshape(2, NP, SLOTS, NA, DEG).transpose(0, 2, 1, 3, 4).reshape(2, 768, DEG)
    pi = order_tables(inverse_legendre, first)
    pi = pi.transpose(0, 2, 1, 3).reshape(2, 768, DEG)
    cube = filter_weight.reshape(16, 2, C, C)
    upper = jnp.concatenate([cube[:, 0], cube[:, 1]], axis=2)
    lower = jnp.concatenate([-cube[:, 1], cube[:, 0]], axis=2)
    kernel = jnp.concatenate([upper, lower], axis=1)

    def middle(modes, adjoint):
        modes = lax.all_to_all(modes.reshape(16, 16, 768), "polar", 0, 0)
        modes = mix(modes, kernel, adjoint)
        return lax.all_to_all(modes, "polar", 0, 0).reshape(DEG, 768)

    modes_g = middle(leg_g(wire_g, pi), True)
    wire_f = lax.all_to_all(dft_f(wire_a, bpt), both, 0, 0)
    modes_f = middle(leg_f(wire_f, pf), False)

    back_g = lax.all_to_all(syn_g(modes_g, pf), both, 0, 0)
    back_f = lax.all_to_all(syn_f(modes_f, pi), both, 0, 0)
    wire_e = lax.all_to_all(idft_g(back_g, bp), "azimuth", 0, 0)
    filtered = idft_f(back_f, bdt)
    return filtered.reshape(ROWS, 24, LON), post(wire_e)


def solution(mesh):
    return jax.shard_map(
        on_device,
        mesh=mesh,
        in_specs=(
            P("polar", "azimuth"),
            P("polar", "azimuth", None),
            P(None, "polar", None),
            P(None, "polar", None),
            P("polar", None),
        ),
        out_specs=(P("polar", "azimuth", None), P("polar", "azimuth")),
        check_vma=False,
    )
```

```python
import functools
import math
import numpy as np
import ml_dtypes
import jax
import jax.numpy as jnp
from jax import lax
from jax.sharding import PartitionSpec as P
from jax.experimental import pallas as pl
from jax.experimental.pallas import tpu as pltpu

LAT = 720
LON = 1440
C = 192
DEG = 256
ORD = 256
ORDER = (0, 7, 6, 5, 4, 1, 3, 2)
NP = 16
NA = 8
ROWS = 45
SLOTS = 6
PAIRS = 90
LP = 96
W = 1152
F32 = jnp.float32
BF = jnp.bfloat16


def params():
    return pltpu.CompilerParams(vmem_limit_bytes=56 << 20)


def dot(a, b, ca, cb):
    return lax.dot_general(a, b, (((ca,), (cb,)), ((), ())), preferred_element_type=F32)


def tables():
    lon = np.arange(LON)[:, None]
    m = np.arange(ORD)[None, :]
    ang = ((lon * m) % LON) * (2.0 * math.pi / LON)
    fac = 1.0 / math.sqrt(LON)
    st = np.stack([np.cos(ang) * fac, -np.sin(ang) * fac], axis=-1).astype(np.float32)
    dbl = np.where(np.arange(ORD) == 0, 1.0, 2.0).astype(np.float32)[None, :, None]
    plain = st.reshape(LON, 2 * ORD).astype(ml_dtypes.bfloat16)
    doubled = (st * dbl).reshape(LON, 2 * ORD).astype(ml_dtypes.bfloat16)
    p4 = plain.reshape(NA, PAIRS, 2, 2 * ORD).transpose(2, 0, 1, 3)
    pp = np.zeros((2, NA, LP, 2 * ORD), ml_dtypes.bfloat16)
    pp[:, :, :PAIRS] = p4
    pp = pp.reshape(2 * NA * LP, 2 * ORD)
    return np.ascontiguousarray(doubled.T), np.ascontiguousarray(pp.T), pp


def prep_body(me_ref, x_ref, *refs):
    outs, s_ref = refs[:8], refs[8]
    step = pl.program_id(0)
    me = me_ref[0]
    lane = lax.broadcasted_iota(jnp.int32, (8, 6144), 1) + step * 6144
    good = lane < PAIRS * 384
    for k in range(SLOTS):
        if k < 5:
            v = x_ref[8 * k:8 * k + 8, :].astype(F32)
        else:
            v = jnp.concatenate([x_ref[40:45, :].astype(F32), jnp.zeros((3, 6144), F32)], 0)
        v = jnp.where(good, v, 0.0)
        for lp in range(16):
            for t in range(3):
                s_ref[3 * k + t, pl.ds(lp, 8, stride=16), :] = v[:, (3 * lp + t) * 128:(3 * lp + t + 1) * 128]
    for s in range(NA):
        row = pl.multiple_of(16 * (me ^ ORDER[s]), 16)
        for q in range(18):
            outs[s][:, q * 128:(q + 1) * 128] = s_ref[q, pl.ds(row, 16), :].astype(BF)


def prep(me, x):
    return pl.pallas_call(
        prep_body,
        grid_spec=pltpu.PrefetchScalarGridSpec(
            num_scalar_prefetch=1,
            grid=(6,),
            in_specs=[pl.BlockSpec((ROWS, 6144), lambda i, me: (0, i))],
            out_specs=[pl.BlockSpec((16, 2304), lambda i, me: (i, 0))] * NA,
            scratch_shapes=[pltpu.VMEM((18, 128, 128), F32)],
        ),
        out_shape=[jax.ShapeDtypeStruct((LP, 2304), BF)] * NA,
        compiler_params=params(),
        name="prep",
    )(me, x)


def post_body(me_ref, *refs):
    r_refs, o_ref, s_ref = refs[:8], refs[8], refs[9]
    me = me_ref[0]
    for s in range(NA):
        row = pl.multiple_of(16 * (me ^ ORDER[s]), 16)
        for q in range(18):
            s_ref[q, pl.ds(row, 16), :] = r_refs[s][:, q * 128:(q + 1) * 128].astype(F32)
    for k in range(SLOTS):
        for lp in range(16):
            for t in range(3):
                v = s_ref[3 * k + t, pl.ds(lp, 8, stride=16), :].astype(BF)
                n = 8 if k < 5 else 5
                o_ref[8 * k:8 * k + n, (3 * lp + t) * 128:(3 * lp + t + 1) * 128] = v[:n]


def post(me, pieces):
    return pl.pallas_call(
        post_body,
        grid_spec=pltpu.PrefetchScalarGridSpec(
            num_scalar_prefetch=1,
            grid=(6,),
            in_specs=[pl.BlockSpec((16, 2304), lambda i, me: (i, 0))] * NA,
            out_specs=pl.BlockSpec((ROWS, 6144), lambda i, me: (0, i)),
            scratch_shapes=[pltpu.VMEM((18, 128, 128), F32)],
        ),
        out_shape=jax.ShapeDtypeStruct((ROWS, LON // NA * C), BF),
        compiler_params=params(),
        name="post",
    )(me, *pieces)


def whole(body, out, *args, scratch=(), name=None):
    return pl.pallas_call(
        body,
        out_shape=jax.ShapeDtypeStruct(out, BF),
        scratch_shapes=list(scratch),
        compiler_params=params(),
        name=name,
    )(*args)


def dft_f_body(me_ref, *refs):
    r_refs, b_ref, o_ref, x_ref = refs[:8], refs[8], refs[9], refs[10]
    me = me_ref[0]
    for s in range(NA):
        row = pl.multiple_of(LP * (me ^ ORDER[s]), 32)
        for k in range(SLOTS):
            v = r_refs[s][:, 384 * k:384 * k + 384]
            x_ref[pl.ds(row, LP), C * k:C * k + C] = v[:, :C]
            x_ref[pl.ds(768 + row, LP), C * k:C * k + C] = v[:, C:]
    y = dot(b_ref[...], x_ref[...], 1, 0).astype(BF)
    o_ref[...] = y.reshape(128, 4, W)


SMEM = pl.BlockSpec(memory_space=pltpu.SMEM)
VMEM = pl.BlockSpec(memory_space=pltpu.VMEM)


def dft_f(me, pieces, bpt):
    return pl.pallas_call(
        dft_f_body,
        in_specs=[SMEM] + [VMEM] * 9,
        out_shape=jax.ShapeDtypeStruct((128, 4, W), BF),
        scratch_shapes=[pltpu.VMEM((1536, W), BF)],
        compiler_params=params(),
        name="dft_f",
    )(me, *pieces, bpt)


def dft_g_body(x_ref, b_ref, o_ref):
    y = dot(b_ref[...], x_ref[...], 1, 1).astype(BF)
    y = jnp.concatenate([y, jnp.zeros((512, W - 1080), BF)], 1)
    o_ref[...] = y.reshape(128, 4, W)


def dft_g(x, bdt):
    return whole(dft_g_body, (128, 4, W), x, bdt, name="dft_g")


def leg_f_body(r_ref, p_ref, o_ref, s_ref):
    for m in range(2):
        for r in range(2):
            v = r_ref[:, 2 * m + r, :]
            for k in range(SLOTS):
                s_ref[128 * k:128 * k + 128, C * r:C * r + C] = v[:, C * k:C * k + C]
        y = dot(p_ref[m], s_ref[...], 0, 0).astype(BF)
        o_ref[:, 384 * m:384 * m + 384] = y


def leg_f(r, pf):
    return whole(leg_f_body, (DEG, 768), r, pf, scratch=[pltpu.VMEM((768, 384), BF)], name="leg_f")


def leg_g_body(r_ref, p_ref, o_ref, s_ref):
    for m in range(2):
        for r in range(2):
            v = r_ref[:, 2 * m + r, :].astype(F32).reshape(NP, NA, W)
            for a in range(NA):
                va = v[:, a, :].astype(BF)
                for t in range(48):
                    s_ref[16 * t:16 * t + 16, C * r + 24 * a:C * r + 24 * a + 24] = va[:, 24 * t:24 * t + 24]
        y = dot(p_ref[m], s_ref[...], 0, 0).astype(BF)
        o_ref[:, 384 * m:384 * m + 384] = y


def leg_g(r, pi):
    return whole(leg_g_body, (DEG, 768), r, pi, scratch=[pltpu.VMEM((768, 384), BF)], name="leg_g")


def mix_body(adjoint, r_ref, k_ref, o_ref, s_ref):
    i = lax.broadcasted_iota(jnp.int32, (256, 256), 0)
    j = lax.broadcasted_iota(jnp.int32, (256, 256), 1)
    perm = ((i // 16 == j % 16) & (i % 16 == j // 16)).astype(F32).astype(BF)
    x = dot(perm, r_ref[...].reshape(256, 768), 1, 0).astype(BF)
    for l in range(16):
        v = x[16 * l:16 * l + 16]
        v = jnp.concatenate([v[:, :384], v[:, 384:]], 0)
        y = dot(v, k_ref[l], 1, 1 if adjoint else 0).astype(BF)
        s_ref[16 * l:16 * l + 16, :384] = y[:16]
        s_ref[16 * l:16 * l + 16, 384:] = y[16:]
    o_ref[...] = dot(perm, s_ref[...], 1, 0).astype(BF).reshape(16, 16, 768)


def mix(r, k, adjoint):
    return whole(functools.partial(mix_body, adjoint), (16, 16, 768), r, k, scratch=[pltpu.VMEM((256, 768), BF)], name="mix_g" if adjoint else "mix_f")


def syn_f_body(x_ref, p_ref, o_ref, z_ref):
    for m in range(2):
        y = dot(p_ref[m], x_ref[:, 384 * m:384 * m + 384], 1, 0).astype(BF)
        for r in range(2):
            for a in range(NA):
                for t in range(48):
                    z_ref[a, :, 24 * t:24 * t + 24] = y[16 * t:16 * t + 16, C * r + 24 * a:C * r + 24 * a + 24]
            for p in range(NP):
                o_ref[8 * p:8 * p + 8, 2 * m + r, :] = z_ref[:, p, :]


def syn_f(x, pi):
    return whole(syn_f_body, (128, 4, W), x, pi, scratch=[pltpu.VMEM((8, 16, W), BF)], name="syn_f")


def syn_g_body(x_ref, p_ref, o_ref, z_ref):
    for m in range(2):
        y = dot(p_ref[m], x_ref[:, 384 * m:384 * m + 384], 1, 0).astype(BF)
        for r in range(2):
            for k in range(SLOTS):
                z_ref[:, C * k:C * k + C] = y[128 * k:128 * k + 128, C * r:C * r + C]
            o_ref[:, 2 * m + r, :] = z_ref[...]


def syn_g(x, pf):
    return whole(syn_g_body, (128, 4, W), x, pf, scratch=[pltpu.VMEM((128, W), BF)], name="syn_g")


def idft_f_body(y_ref, b_ref, o_ref):
    y = y_ref[...].reshape(512, W)
    o_ref[...] = dot(y[:, :1080], b_ref[...], 0, 0).astype(BF)


def idft_f(y, bdt):
    return whole(idft_f_body, (1080, LON), y, bdt, name="idft_f")


def idft_g_body(me_ref, y_ref, b_ref, *refs):
    outs, z_ref = refs[:8], refs[8]
    me = me_ref[0]
    y = y_ref[...].reshape(512, W)
    z_ref[...] = dot(b_ref[...], y, 1, 0).astype(BF)
    for s in range(NA):
        row = pl.multiple_of(LP * (me ^ ORDER[s]), 32)
        for k in range(SLOTS):
            e = z_ref[pl.ds(row, LP), C * k:C * k + C]
            o = z_ref[pl.ds(768 + row, LP), C * k:C * k + C]
            outs[s][:, 384 * k:384 * k + 384] = jnp.concatenate([e, o], 1)


def idft_g(me, y, bp):
    return pl.pallas_call(
        idft_g_body,
        in_specs=[SMEM, VMEM, VMEM],
        out_shape=[jax.ShapeDtypeStruct((LP, 2304), BF)] * NA,
        out_specs=[VMEM] * NA,
        scratch_shapes=[pltpu.VMEM((1536, W), BF)],
        compiler_params=params(),
        name="idft_g",
    )(me, y, bp)


def order_tables(table, first):
    part = lax.dynamic_slice(table, (0, first, 0), (LAT, 2, DEG))
    part = part.reshape(NP, ROWS, 2, DEG).transpose(2, 0, 1, 3)
    return jnp.pad(part, ((0, 0), (0, 0), (0, 3), (0, 0)))


def hop(piece, i):
    s = ORDER[i]
    return lax.ppermute(piece, "azimuth", [(a, a ^ s) for a in range(NA)])


def fence(*values):
    return lax.optimization_barrier(values)


def on_device(grid_input, cotangent, forward_legendre, inverse_legendre, filter_weight):
    bdt, bpt, bp = [jnp.asarray(t) for t in tables()]
    both = ("polar", "azimuth")
    me = lax.axis_index("azimuth")[None]
    first = 2 * me[0]

    def over_all(x):
        return lax.all_to_all(x, both, 0, 0)

    def over_polar(x):
        return lax.all_to_all(x, "polar", 0, 0)

    pieces = prep(me, grid_input)
    got = [pieces[0]] + [hop(pieces[i], i) for i in range(1, NA)]

    pf = order_tables(forward_legendre, first)
    pf = pf.reshape(2, NP, SLOTS, NA, DEG).transpose(0, 2, 1, 3, 4).reshape(2, 768, DEG)
    pi = order_tables(inverse_legendre, first)
    pi = pi.transpose(0, 2, 1, 3).reshape(2, 768, DEG)
    cube = filter_weight.reshape(16, 2, C, C)
    upper = jnp.concatenate([cube[:, 0], cube[:, 1]], axis=2)
    lower = jnp.concatenate([-cube[:, 1], cube[:, 0]], axis=2)
    kernel = jnp.concatenate([upper, lower], axis=1)
    wire_g = over_all(dft_g(cotangent.reshape(1080, LON), bdt))
    wire_g, kernel, pf, pi, got[1], got[2] = fence(wire_g, kernel, pf, pi, got[1], got[2])
    modes_g = leg_g(wire_g, pi)
    modes_g, got[0] = fence(modes_g, got[0])
    coef_g = over_polar(modes_g.reshape(16, 16, 768))

    wire_f = dft_f(me, got, bpt)
    wire_f, coef_g = fence(wire_f, coef_g)
    wire_f = over_all(wire_f)
    mixed_g = over_polar(mix(coef_g, kernel, True)).reshape(DEG, 768)
    coef_f = over_polar(leg_f(wire_f, pf).reshape(16, 16, 768))

    back_g = over_all(syn_g(mixed_g, pf))
    mixed_f = over_polar(mix(coef_f, kernel, False)).reshape(DEG, 768)
    pieces = idft_g(me, back_g, bp)
    got = [pieces[0]] + [hop(pieces[i], i) for i in range(1, NA)]
    mixed_f, got[1], got[2] = fence(mixed_f, got[1], got[2])
    wire = syn_f(mixed_f, pi)
    back_f = over_all(wire)
    filtered = idft_f(back_f, bdt)
    filtered, got[0] = fence(filtered, got[0])
    return filtered.reshape(ROWS, 24, LON), post(me, got)


def solution(mesh):
    return jax.shard_map(
        on_device,
        mesh=mesh,
        in_specs=(
            P("polar", "azimuth"),
            P("polar", "azimuth", None),
            P(None, "polar", None),
            P(None, "polar", None),
            P("polar", None),
        ),
        out_specs=(P("polar", "azimuth", None), P("polar", "azimuth")),
        check_vma=False,
    )
```

```python
import functools
import math
import numpy as np
import ml_dtypes
import jax
import jax.numpy as jnp
from jax import lax
from jax.sharding import PartitionSpec as P
from jax.experimental import pallas as pl
from jax.experimental.pallas import tpu as pltpu

LAT = 720
LON = 1440
C = 192
DEG = 256
ORD = 256
ORDER_A = (0, 1, 3, 7, 6, 5, 4, 2)
ORDER_E = (0, 7, 6, 1, 3, 5, 4, 2)
NP = 16
NA = 8
ROWS = 45
SLOTS = 6
PAIRS = 90
LP = 96
W = 1152
F32 = jnp.float32
BF = jnp.bfloat16


def params():
    return pltpu.CompilerParams(vmem_limit_bytes=56 << 20)


def dot(a, b, ca, cb):
    return lax.dot_general(a, b, (((ca,), (cb,)), ((), ())), preferred_element_type=F32)


def tables():
    lon = np.arange(LON)[:, None]
    m = np.arange(ORD)[None, :]
    ang = ((lon * m) % LON) * (2.0 * math.pi / LON)
    fac = 1.0 / math.sqrt(LON)
    st = np.stack([np.cos(ang) * fac, -np.sin(ang) * fac], axis=-1).astype(np.float32)
    dbl = np.where(np.arange(ORD) == 0, 1.0, 2.0).astype(np.float32)[None, :, None]
    plain = st.reshape(LON, 2 * ORD).astype(ml_dtypes.bfloat16)
    doubled = (st * dbl).reshape(LON, 2 * ORD).astype(ml_dtypes.bfloat16)
    p4 = plain.reshape(NA, PAIRS, 2, 2 * ORD).transpose(2, 0, 1, 3)
    pp = np.zeros((2, NA, LP, 2 * ORD), ml_dtypes.bfloat16)
    pp[:, :, :PAIRS] = p4
    pp = pp.reshape(2 * NA * LP, 2 * ORD)
    return np.ascontiguousarray(doubled.T), np.ascontiguousarray(pp.T), pp


def prep_body(me_ref, x_ref, *refs):
    outs, s_ref = refs[:8], refs[8]
    step = pl.program_id(0)
    me = me_ref[0]
    lane = lax.broadcasted_iota(jnp.int32, (8, 6144), 1) + step * 6144
    good = lane < PAIRS * 384
    for k in range(SLOTS):
        if k < 5:
            v = x_ref[8 * k:8 * k + 8, :].astype(F32)
        else:
            v = jnp.concatenate([x_ref[40:45, :].astype(F32), jnp.zeros((3, 6144), F32)], 0)
        v = jnp.where(good, v, 0.0)
        for lp in range(16):
            for t in range(3):
                s_ref[3 * k + t, pl.ds(lp, 8, stride=16), :] = v[:, (3 * lp + t) * 128:(3 * lp + t + 1) * 128]
    for s in range(NA):
        row = pl.multiple_of(16 * (me ^ ORDER_A[s]), 16)
        for q in range(18):
            outs[s][:, q * 128:(q + 1) * 128] = s_ref[q, pl.ds(row, 16), :].astype(BF)


def prep(me, x):
    return pl.pallas_call(
        prep_body,
        grid_spec=pltpu.PrefetchScalarGridSpec(
            num_scalar_prefetch=1,
            grid=(6,),
            in_specs=[pl.BlockSpec((ROWS, 6144), lambda i, me: (0, i))],
            out_specs=[pl.BlockSpec((16, 2304), lambda i, me: (i, 0))] * NA,
            scratch_shapes=[pltpu.VMEM((18, 128, 128), F32)],
        ),
        out_shape=[jax.ShapeDtypeStruct((LP, 2304), BF)] * NA,
        compiler_params=params(),
        name="prep",
    )(me, x)


def post_body(me_ref, *refs):
    r_refs, o_ref, s_ref = refs[:8], refs[8], refs[9]
    me = me_ref[0]
    for s in range(NA):
        row = pl.multiple_of(16 * (me ^ ORDER_E[s]), 16)
        for q in range(18):
            s_ref[q, pl.ds(row, 16), :] = r_refs[s][:, q * 128:(q + 1) * 128].astype(F32)
    for k in range(SLOTS):
        for lp in range(16):
            for t in range(3):
                v = s_ref[3 * k + t, pl.ds(lp, 8, stride=16), :].astype(BF)
                n = 8 if k < 5 else 5
                o_ref[8 * k:8 * k + n, (3 * lp + t) * 128:(3 * lp + t + 1) * 128] = v[:n]


def post(me, pieces):
    return pl.pallas_call(
        post_body,
        grid_spec=pltpu.PrefetchScalarGridSpec(
            num_scalar_prefetch=1,
            grid=(6,),
            in_specs=[pl.BlockSpec((16, 2304), lambda i, me: (i, 0))] * NA,
            out_specs=pl.BlockSpec((ROWS, 6144), lambda i, me: (0, i)),
            scratch_shapes=[pltpu.VMEM((18, 128, 128), F32)],
        ),
        out_shape=jax.ShapeDtypeStruct((ROWS, LON // NA * C), BF),
        compiler_params=params(),
        name="post",
    )(me, *pieces)


def whole(body, out, *args, scratch=(), name=None):
    return pl.pallas_call(
        body,
        out_shape=jax.ShapeDtypeStruct(out, BF),
        scratch_shapes=list(scratch),
        compiler_params=params(),
        name=name,
    )(*args)


def dft_f_body(me_ref, *refs):
    r_refs, b_ref, o_ref, x_ref = refs[:8], refs[8], refs[9], refs[10]
    me = me_ref[0]
    for s in range(NA):
        row = pl.multiple_of(LP * (me ^ ORDER_A[s]), 32)
        for k in range(SLOTS):
            v = r_refs[s][:, 384 * k:384 * k + 384]
            x_ref[pl.ds(row, LP), C * k:C * k + C] = v[:, :C]
            x_ref[pl.ds(768 + row, LP), C * k:C * k + C] = v[:, C:]
    y = dot(b_ref[...], x_ref[...], 1, 0).astype(BF)
    o_ref[...] = y.reshape(128, 4, W)


SMEM = pl.BlockSpec(memory_space=pltpu.SMEM)
VMEM = pl.BlockSpec(memory_space=pltpu.VMEM)


def dft_f(me, pieces, bpt):
    return pl.pallas_call(
        dft_f_body,
        in_specs=[SMEM] + [VMEM] * 9,
        out_shape=jax.ShapeDtypeStruct((128, 4, W), BF),
        scratch_shapes=[pltpu.VMEM((1536, W), BF)],
        compiler_params=params(),
        name="dft_f",
    )(me, *pieces, bpt)


def dft_g_body(x_ref, b_ref, o_ref):
    y = dot(b_ref[...], x_ref[...], 1, 1).astype(BF)
    y = jnp.concatenate([y, jnp.zeros((512, W - 1080), BF)], 1)
    o_ref[...] = y.reshape(128, 4, W)


def dft_g(x, bdt):
    return whole(dft_g_body, (128, 4, W), x, bdt, name="dft_g")


def leg_f_body(r_ref, p_ref, o_ref, s_ref):
    for m in range(2):
        for r in range(2):
            v = r_ref[:, 2 * m + r, :]
            for k in range(SLOTS):
                s_ref[128 * k:128 * k + 128, C * r:C * r + C] = v[:, C * k:C * k + C]
        y = dot(p_ref[m], s_ref[...], 0, 0).astype(BF)
        o_ref[:, 384 * m:384 * m + 384] = y


def leg_f(r, pf):
    return whole(leg_f_body, (DEG, 768), r, pf, scratch=[pltpu.VMEM((768, 384), BF)], name="leg_f")


def leg_g_body(r_ref, p_ref, o_ref, s_ref):
    for m in range(2):
        for r in range(2):
            v = r_ref[:, 2 * m + r, :].astype(F32).reshape(NP, NA, W)
            for a in range(NA):
                va = v[:, a, :].astype(BF)
                for t in range(48):
                    s_ref[16 * t:16 * t + 16, C * r + 24 * a:C * r + 24 * a + 24] = va[:, 24 * t:24 * t + 24]
        y = dot(p_ref[m], s_ref[...], 0, 0).astype(BF)
        o_ref[:, 384 * m:384 * m + 384] = y


def leg_g(r, pi):
    return whole(leg_g_body, (DEG, 768), r, pi, scratch=[pltpu.VMEM((768, 384), BF)], name="leg_g")


def mix_body(adjoint, r_ref, k_ref, o_ref, s_ref):
    i = lax.broadcasted_iota(jnp.int32, (256, 256), 0)
    j = lax.broadcasted_iota(jnp.int32, (256, 256), 1)
    perm = ((i // 16 == j % 16) & (i % 16 == j // 16)).astype(F32).astype(BF)
    x = dot(perm, r_ref[...].reshape(256, 768), 1, 0).astype(BF)
    for l in range(16):
        v = x[16 * l:16 * l + 16]
        v = jnp.concatenate([v[:, :384], v[:, 384:]], 0)
        y = dot(v, k_ref[l], 1, 1 if adjoint else 0).astype(BF)
        s_ref[16 * l:16 * l + 16, :384] = y[:16]
        s_ref[16 * l:16 * l + 16, 384:] = y[16:]
    o_ref[...] = dot(perm, s_ref[...], 1, 0).astype(BF).reshape(16, 16, 768)


def mix(r, k, adjoint):
    return whole(functools.partial(mix_body, adjoint), (16, 16, 768), r, k, scratch=[pltpu.VMEM((256, 768), BF)], name="mix_g" if adjoint else "mix_f")


def syn_f_body(x_ref, p_ref, o_ref, z_ref):
    for m in range(2):
        y = dot(p_ref[m], x_ref[:, 384 * m:384 * m + 384], 1, 0).astype(BF)
        for r in range(2):
            for a in range(NA):
                for t in range(48):
                    z_ref[a, :, 24 * t:24 * t + 24] = y[16 * t:16 * t + 16, C * r + 24 * a:C * r + 24 * a + 24]
            for p in range(NP):
                o_ref[8 * p:8 * p + 8, 2 * m + r, :] = z_ref[:, p, :]


def syn_f(x, pi):
    return whole(syn_f_body, (128, 4, W), x, pi, scratch=[pltpu.VMEM((8, 16, W), BF)], name="syn_f")


def syn_g_body(x_ref, p_ref, o_ref, z_ref):
    for m in range(2):
        y = dot(p_ref[m], x_ref[:, 384 * m:384 * m + 384], 1, 0).astype(BF)
        for r in range(2):
            for k in range(SLOTS):
                z_ref[:, C * k:C * k + C] = y[128 * k:128 * k + 128, C * r:C * r + C]
            o_ref[:, 2 * m + r, :] = z_ref[...]


def syn_g(x, pf):
    return whole(syn_g_body, (128, 4, W), x, pf, scratch=[pltpu.VMEM((128, W), BF)], name="syn_g")


def idft_f_body(y_ref, b_ref, o_ref):
    y = y_ref[...].reshape(512, W)
    o_ref[...] = dot(y[:, :1080], b_ref[...], 0, 0).astype(BF)


def idft_f(y, bdt):
    return whole(idft_f_body, (1080, LON), y, bdt, name="idft_f")


def idft_g_body(me_ref, y_ref, b_ref, *refs):
    outs, z_ref = refs[:8], refs[8]
    me = me_ref[0]
    y = y_ref[...].reshape(512, W)
    z_ref[...] = dot(b_ref[...], y, 1, 0).astype(BF)
    for s in range(NA):
        row = pl.multiple_of(LP * (me ^ ORDER_E[s]), 32)
        for k in range(SLOTS):
            e = z_ref[pl.ds(row, LP), C * k:C * k + C]
            o = z_ref[pl.ds(768 + row, LP), C * k:C * k + C]
            outs[s][:, 384 * k:384 * k + 384] = jnp.concatenate([e, o], 1)


def idft_g(me, y, bp):
    return pl.pallas_call(
        idft_g_body,
        in_specs=[SMEM, VMEM, VMEM],
        out_shape=[jax.ShapeDtypeStruct((LP, 2304), BF)] * NA,
        out_specs=[VMEM] * NA,
        scratch_shapes=[pltpu.VMEM((1536, W), BF)],
        compiler_params=params(),
        name="idft_g",
    )(me, y, bp)


def order_tables(table, first):
    part = lax.dynamic_slice(table, (0, first, 0), (LAT, 2, DEG))
    part = part.reshape(NP, ROWS, 2, DEG).transpose(2, 0, 1, 3)
    return jnp.pad(part, ((0, 0), (0, 0), (0, 3), (0, 0)))


def hops(pieces, order):
    def hop(piece, s):
        return lax.ppermute(piece, "azimuth", [(a, a ^ s) for a in range(NA)])

    return [pieces[0]] + [hop(pieces[i], order[i]) for i in range(1, NA)]


def fence(*values):
    return lax.optimization_barrier(values)


def on_device(grid_input, cotangent, forward_legendre, inverse_legendre, filter_weight):
    bdt, bpt, bp = [jnp.asarray(t) for t in tables()]
    both = ("polar", "azimuth")
    me = lax.axis_index("azimuth")[None]
    first = 2 * me[0]

    def over_all(x):
        return lax.all_to_all(x, both, 0, 0)

    def over_polar(x):
        return lax.all_to_all(x, "polar", 0, 0)

    pieces = list(prep(me, grid_input))
    got = hops(pieces, ORDER_A)

    pf = order_tables(forward_legendre, first)
    pf = pf.reshape(2, NP, SLOTS, NA, DEG).transpose(0, 2, 1, 3, 4).reshape(2, 768, DEG)
    pi = order_tables(inverse_legendre, first)
    pi = pi.transpose(0, 2, 1, 3).reshape(2, 768, DEG)
    cube = filter_weight.reshape(16, 2, C, C)
    upper = jnp.concatenate([cube[:, 0], cube[:, 1]], axis=2)
    lower = jnp.concatenate([-cube[:, 1], cube[:, 0]], axis=2)
    kernel = jnp.concatenate([upper, lower], axis=1)

    cot = cotangent.reshape(1080, LON)
    cot, got[0] = fence(cot, got[0])
    wire_g = over_all(dft_g(cot, bdt))
    wire_g, kernel, pf, pi, got[1], got[2] = fence(wire_g, kernel, pf, pi, got[1], got[2])
    modes_g = leg_g(wire_g, pi)
    modes_g, got[3], got[4] = fence(modes_g, got[3], got[4])
    coef_g = over_polar(modes_g.reshape(16, 16, 768))
    coef_g, got[5] = fence(coef_g, got[5])
    mixed_g = mix(coef_g, kernel, True)
    mixed_g, got[0] = fence(mixed_g, got[0])
    mixed_g = over_polar(mixed_g).reshape(DEG, 768)
    wire_f = over_all(dft_f(me, got, bpt))

    back_g = over_all(syn_g(mixed_g, pf))
    modes_f = leg_f(wire_f, pf)
    modes_f, back_g = fence(modes_f, back_g)
    coef_f = over_polar(modes_f.reshape(16, 16, 768))

    pieces = list(idft_g(me, back_g, bp))
    pieces[0], coef_f = fence(pieces[0], coef_f)
    mixed_f = over_polar(mix(coef_f, kernel, False)).reshape(DEG, 768)
    got = hops(pieces, ORDER_E)
    mixed_f, got[1], got[2], got[3], got[4] = fence(mixed_f, got[1], got[2], got[3], got[4])
    back_f = over_all(syn_f(mixed_f, pi))
    filtered = idft_f(back_f, bdt)
    filtered, got[0] = fence(filtered, got[0])
    return filtered.reshape(ROWS, 24, LON), post(me, got)


def solution(mesh):
    return jax.shard_map(
        on_device,
        mesh=mesh,
        in_specs=(
            P("polar", "azimuth"),
            P("polar", "azimuth", None),
            P(None, "polar", None),
            P(None, "polar", None),
            P("polar", None),
        ),
        out_specs=(P("polar", "azimuth", None), P("polar", "azimuth")),
        check_vma=False,
    )
```

```python
import functools
import math
import numpy as np
import ml_dtypes
import jax
import jax.numpy as jnp
from jax import lax
from jax.sharding import PartitionSpec as P
from jax.experimental import pallas as pl
from jax.experimental.pallas import tpu as pltpu

LAT = 720
LON = 1440
C = 192
DEG = 256
ORD = 256
ORDER = (0, 7, 6, 5, 4, 2, 3, 1)
ORDER_E = (0, 2, 3, 1, 7, 6, 5, 4)
NP = 16
NA = 8
ROWS = 45
SLOTS = 6
PAIRS = 90
LP = 96
W = 1152
F32 = jnp.float32
BF = jnp.bfloat16


def params():
    return pltpu.CompilerParams(vmem_limit_bytes=56 << 20)


def dot(a, b, ca, cb):
    return lax.dot_general(a, b, (((ca,), (cb,)), ((), ())), preferred_element_type=F32)


def tables():
    lon = np.arange(LON)[:, None]
    m = np.arange(ORD)[None, :]
    ang = ((lon * m) % LON) * (2.0 * math.pi / LON)
    fac = 1.0 / math.sqrt(LON)
    st = np.stack([np.cos(ang) * fac, -np.sin(ang) * fac], axis=-1).astype(np.float32)
    dbl = np.where(np.arange(ORD) == 0, 1.0, 2.0).astype(np.float32)[None, :, None]
    plain = st.reshape(LON, 2 * ORD).astype(ml_dtypes.bfloat16)
    doubled = (st * dbl).reshape(LON, 2 * ORD).astype(ml_dtypes.bfloat16)
    p4 = plain.reshape(NA, PAIRS, 2, 2 * ORD).transpose(2, 0, 1, 3)
    pp = np.zeros((2, NA, LP, 2 * ORD), ml_dtypes.bfloat16)
    pp[:, :, :PAIRS] = p4
    pp = pp.reshape(2 * NA * LP, 2 * ORD)
    return np.ascontiguousarray(doubled.T), np.ascontiguousarray(pp.T), pp


def prep_body(me_ref, x_ref, *refs):
    outs, s_ref = refs[:8], refs[8]
    step = pl.program_id(0)
    me = me_ref[0]
    lane = lax.broadcasted_iota(jnp.int32, (8, 6144), 1) + step * 6144
    good = lane < PAIRS * 384
    for k in range(SLOTS):
        if k < 5:
            v = x_ref[8 * k:8 * k + 8, :].astype(F32)
        else:
            v = jnp.concatenate([x_ref[40:45, :].astype(F32), jnp.zeros((3, 6144), F32)], 0)
        v = jnp.where(good, v, 0.0)
        for lp in range(16):
            for t in range(3):
                s_ref[3 * k + t, pl.ds(lp, 8, stride=16), :] = v[:, (3 * lp + t) * 128:(3 * lp + t + 1) * 128]
    for s in range(NA):
        row = pl.multiple_of(16 * (me ^ ORDER[s]), 16)
        for q in range(18):
            outs[s][:, q * 128:(q + 1) * 128] = s_ref[q, pl.ds(row, 16), :].astype(BF)


def prep(me, x):
    return pl.pallas_call(
        prep_body,
        grid_spec=pltpu.PrefetchScalarGridSpec(
            num_scalar_prefetch=1,
            grid=(6,),
            in_specs=[pl.BlockSpec((ROWS, 6144), lambda i, me: (0, i))],
            out_specs=[pl.BlockSpec((16, 2304), lambda i, me: (i, 0))] * NA,
            scratch_shapes=[pltpu.VMEM((18, 128, 128), F32)],
        ),
        out_shape=[jax.ShapeDtypeStruct((LP, 2304), BF)] * NA,
        compiler_params=params(),
        name="prep",
    )(me, x)


def post_body(me_ref, *refs):
    r_refs, o_ref, s_ref = refs[:8], refs[8], refs[9]
    me = me_ref[0]
    for s in range(NA):
        row = pl.multiple_of(16 * (me ^ ORDER_E[s]), 16)
        for q in range(18):
            s_ref[q, pl.ds(row, 16), :] = r_refs[s][:, q * 128:(q + 1) * 128].astype(F32)
    for k in range(SLOTS):
        for lp in range(16):
            for t in range(3):
                v = s_ref[3 * k + t, pl.ds(lp, 8, stride=16), :].astype(BF)
                n = 8 if k < 5 else 5
                o_ref[8 * k:8 * k + n, (3 * lp + t) * 128:(3 * lp + t + 1) * 128] = v[:n]


def post(me, pieces):
    return pl.pallas_call(
        post_body,
        grid_spec=pltpu.PrefetchScalarGridSpec(
            num_scalar_prefetch=1,
            grid=(6,),
            in_specs=[pl.BlockSpec((16, 2304), lambda i, me: (i, 0))] * NA,
            out_specs=pl.BlockSpec((ROWS, 6144), lambda i, me: (0, i)),
            scratch_shapes=[pltpu.VMEM((18, 128, 128), F32)],
        ),
        out_shape=jax.ShapeDtypeStruct((ROWS, LON // NA * C), BF),
        compiler_params=params(),
        name="post",
    )(me, *pieces)


def whole(body, out, *args, scratch=(), name=None):
    return pl.pallas_call(
        body,
        out_shape=jax.ShapeDtypeStruct(out, BF),
        scratch_shapes=list(scratch),
        compiler_params=params(),
        name=name,
    )(*args)


def dft_f_body(me_ref, *refs):
    r_refs, b_ref, g_ref, o_ref, x_ref = refs[:8], *refs[8:]
    me = me_ref[0]
    for s in range(NA):
        row = pl.multiple_of(LP * (me ^ ORDER[s]), 32)
        for k in range(SLOTS):
            v = r_refs[s][:, 384 * k:384 * k + 384]
            x_ref[pl.ds(row, LP), C * k:C * k + C] = v[:, :C]
            x_ref[pl.ds(768 + row, LP), C * k:C * k + C] = v[:, C:]
    y = dot(b_ref[...], x_ref[...], 1, 0).astype(BF)
    o_ref[:, :4, :] = y.reshape(128, 4, W)
    o_ref[:, 4:, :] = g_ref[...]


SMEM = pl.BlockSpec(memory_space=pltpu.SMEM)
VMEM = pl.BlockSpec(memory_space=pltpu.VMEM)


def dft_f(me, pieces, bpt, wire_g):
    return pl.pallas_call(
        dft_f_body,
        in_specs=[SMEM] + [VMEM] * 10,
        out_shape=jax.ShapeDtypeStruct((128, 8, W), BF),
        scratch_shapes=[pltpu.VMEM((1536, W), BF)],
        compiler_params=params(),
        name="dft_f",
    )(me, *pieces, bpt, wire_g)


def dft_g_body(x_ref, b_ref, o_ref):
    y = dot(b_ref[...], x_ref[...], 1, 1).astype(BF)
    y = jnp.concatenate([y, jnp.zeros((512, W - 1080), BF)], 1)
    o_ref[...] = y.reshape(128, 4, W)


def dft_g(x, bdt):
    return whole(dft_g_body, (128, 4, W), x, bdt, name="dft_g")


def leg_body(r_ref, pf_ref, pi_ref, o_ref, s_ref, t_ref):
    for m in range(2):
        for r in range(2):
            v = r_ref[:, 2 * m + r, :]
            for k in range(SLOTS):
                s_ref[m, 128 * k:128 * k + 128, C * r:C * r + C] = v[:, C * k:C * k + C]
            v = r_ref[:, 4 + 2 * m + r, :].astype(F32).reshape(NP, NA, W)
            for a in range(NA):
                va = v[:, a, :].astype(BF)
                for t in range(48):
                    t_ref[m, 16 * t:16 * t + 16, C * r + 24 * a:C * r + 24 * a + 24] = va[:, 24 * t:24 * t + 24]
        o_ref[:, 384 * m:384 * m + 384] = dot(pf_ref[m], s_ref[m], 0, 0).astype(BF)
        o_ref[:, 768 + 384 * m:768 + 384 * m + 384] = dot(pi_ref[m], t_ref[m], 0, 0).astype(BF)


def leg(r, pf, pi):
    return whole(leg_body, (DEG, 1536), r, pf, pi, scratch=[pltpu.VMEM((2, 768, 384), BF)] * 2, name="leg")


def mix_body(r_ref, k_ref, o_ref, s_ref):
    i = lax.broadcasted_iota(jnp.int32, (256, 256), 0)
    j = lax.broadcasted_iota(jnp.int32, (256, 256), 1)
    perm = ((i // 16 == j % 16) & (i % 16 == j // 16)).astype(F32).astype(BF)
    x = dot(perm, r_ref[...].reshape(256, 1536), 1, 0).astype(BF)
    for l in range(16):
        for side in range(2):
            v = x[16 * l:16 * l + 16, 768 * side:768 * side + 768]
            v = jnp.concatenate([v[:, :384], v[:, 384:]], 0)
            y = dot(v, k_ref[l], 1, side).astype(BF)
            s_ref[16 * l:16 * l + 16, 768 * side:768 * side + 384] = y[:16]
            s_ref[16 * l:16 * l + 16, 768 * side + 384:768 * side + 768] = y[16:]
    o_ref[...] = dot(perm, s_ref[...], 1, 0).astype(BF).reshape(16, 16, 1536)


def mix(r, k):
    return whole(mix_body, (16, 16, 1536), r, k, scratch=[pltpu.VMEM((256, 1536), BF)], name="mix")


def syn_body(x_ref, pf_ref, pi_ref, o_ref, z_ref, y_ref):
    for m in range(2):
        y = dot(pi_ref[m], x_ref[:, 384 * m:384 * m + 384], 1, 0).astype(BF)
        for r in range(2):
            for a in range(NA):
                for t in range(48):
                    z_ref[a, :, 24 * t:24 * t + 24] = y[16 * t:16 * t + 16, C * r + 24 * a:C * r + 24 * a + 24]
            for p in range(NP):
                o_ref[8 * p:8 * p + 8, 2 * m + r, :] = z_ref[:, p, :]
        y = dot(pf_ref[m], x_ref[:, 768 + 384 * m:768 + 384 * m + 384], 1, 0).astype(BF)
        for r in range(2):
            for k in range(SLOTS):
                y_ref[:, C * k:C * k + C] = y[128 * k:128 * k + 128, C * r:C * r + C]
            o_ref[:, 4 + 2 * m + r, :] = y_ref[...]


def syn(x, pf, pi):
    return whole(syn_body, (128, 8, W), x, pf, pi, scratch=[pltpu.VMEM((8, 16, W), BF), pltpu.VMEM((128, W), BF)], name="syn")


def idft_f_body(y_ref, b_ref, o_ref):
    y = y_ref[:, :4, :].reshape(512, W)
    o_ref[...] = dot(y[:, :1080], b_ref[...], 0, 0).astype(BF)


def idft_f(y, bdt):
    return whole(idft_f_body, (1080, LON), y, bdt, name="idft_f")


def idft_g_body(me_ref, y_ref, b_ref, *refs):
    outs, z_ref = refs[:8], refs[8]
    me = me_ref[0]
    y = y_ref[:, 4:, :].reshape(512, W)
    z_ref[...] = dot(b_ref[...], y, 1, 0).astype(BF)
    for s in range(NA):
        row = pl.multiple_of(LP * (me ^ ORDER_E[s]), 32)
        for k in range(SLOTS):
            e = z_ref[pl.ds(row, LP), C * k:C * k + C]
            o = z_ref[pl.ds(768 + row, LP), C * k:C * k + C]
            outs[s][:, 384 * k:384 * k + 384] = jnp.concatenate([e, o], 1)


def idft_g(me, y, bp):
    return pl.pallas_call(
        idft_g_body,
        in_specs=[SMEM, VMEM, VMEM],
        out_shape=[jax.ShapeDtypeStruct((LP, 2304), BF)] * NA,
        out_specs=[VMEM] * NA,
        scratch_shapes=[pltpu.VMEM((1536, W), BF)],
        compiler_params=params(),
        name="idft_g",
    )(me, y, bp)


def order_tables(table, first):
    part = lax.dynamic_slice(table, (0, first, 0), (LAT, 2, DEG))
    part = part.reshape(NP, ROWS, 2, DEG).transpose(2, 0, 1, 3)
    return jnp.pad(part, ((0, 0), (0, 0), (0, 3), (0, 0)))


def hops(pieces, order):
    def hop(piece, s):
        return lax.ppermute(piece, "azimuth", [(a, a ^ s) for a in range(NA)])

    return [pieces[0]] + [hop(pieces[i], order[i]) for i in range(1, NA)]


def fence(*values):
    return lax.optimization_barrier(values)


def on_device(grid_input, cotangent, forward_legendre, inverse_legendre, filter_weight):
    bdt, bpt, bp = [jnp.asarray(t) for t in tables()]
    both = ("polar", "azimuth")
    me = lax.axis_index("azimuth")[None]
    first = 2 * me[0]

    def over_all(x):
        return lax.all_to_all(x, both, 0, 0)

    def over_polar(x):
        return lax.all_to_all(x, "polar", 0, 0)

    pieces = list(prep(me, grid_input))
    got = hops(pieces, ORDER)

    pf = order_tables(forward_legendre, first)
    pf = pf.reshape(2, NP, SLOTS, NA, DEG).transpose(0, 2, 1, 3, 4).reshape(2, 768, DEG)
    pi = order_tables(inverse_legendre, first)
    pi = pi.transpose(0, 2, 1, 3).reshape(2, 768, DEG)
    cube = filter_weight.reshape(16, 2, C, C)
    upper = jnp.concatenate([cube[:, 0], cube[:, 1]], axis=2)
    lower = jnp.concatenate([-cube[:, 1], cube[:, 0]], axis=2)
    kernel = jnp.concatenate([upper, lower], axis=1)

    cot = cotangent.reshape(1080, LON)
    cot, got[0] = fence(cot, got[0])
    wire = dft_f(me, got, bpt, dft_g(cot, bdt))
    modes = leg(over_all(wire), pf, pi)
    modes = over_polar(modes.reshape(16, 16, 1536))
    modes = over_polar(mix(modes, kernel)).reshape(DEG, 1536)
    back = over_all(syn(modes, pf, pi))

    got = hops(list(idft_g(me, back, bp)), ORDER_E)
    filtered = idft_f(back, bdt)
    filtered, *got = fence(filtered, *got)
    return filtered.reshape(ROWS, 24, LON), post(me, got)


def solution(mesh):
    return jax.shard_map(
        on_device,
        mesh=mesh,
        in_specs=(
            P("polar", "azimuth"),
            P("polar", "azimuth", None),
            P(None, "polar", None),
            P(None, "polar", None),
            P("polar", None),
        ),
        out_specs=(P("polar", "azimuth", None), P("polar", "azimuth")),
        check_vma=False,
    )
```

```python
import functools
import math
import numpy as np
import ml_dtypes
import jax
import jax.numpy as jnp
from jax import lax
from jax.sharding import PartitionSpec as P
from jax.experimental import pallas as pl
from jax.experimental.pallas import tpu as pltpu

LAT = 720
LON = 1440
C = 192
DEG = 256
ORD = 256
NP = 16
NA = 8
ROWS = 45
SLOTS = 6
PAIRS = 90
LP = 96
W = 1152
F32 = jnp.float32
BF = jnp.bfloat16


def params():
    return pltpu.CompilerParams(vmem_limit_bytes=24 << 20)


def dot(a, b, ca, cb):
    return lax.dot_general(a, b, (((ca,), (cb,)), ((), ())), preferred_element_type=F32)


def tables():
    lon = np.arange(LON)[:, None]
    m = np.arange(ORD)[None, :]
    ang = ((lon * m) % LON) * (2.0 * math.pi / LON)
    fac = 1.0 / math.sqrt(LON)
    st = np.stack([np.cos(ang) * fac, -np.sin(ang) * fac], axis=-1).astype(np.float32)
    dbl = np.where(np.arange(ORD) == 0, 1.0, 2.0).astype(np.float32)[None, :, None]
    plain = st.reshape(LON, 2 * ORD).astype(ml_dtypes.bfloat16)
    doubled = (st * dbl).reshape(LON, 2 * ORD).astype(ml_dtypes.bfloat16)
    p4 = plain.reshape(NA, PAIRS, 2, 2 * ORD).transpose(2, 0, 1, 3)
    pp = np.zeros((2, NA, LP, 2 * ORD), ml_dtypes.bfloat16)
    pp[:, :, :PAIRS] = p4
    pp = pp.reshape(2 * NA * LP, 2 * ORD)
    return np.ascontiguousarray(doubled.T), np.ascontiguousarray(pp.T), pp


SMEM = pl.BlockSpec(memory_space=pltpu.SMEM)
VMEM = pl.BlockSpec(memory_space=pltpu.VMEM)


def near(x):
    return pltpu.with_memory_space_constraint(x, pltpu.VMEM)


def prep_body(x_ref, o_ref, s_ref):
    step = pl.program_id(0)
    lane = lax.broadcasted_iota(jnp.int32, (8, 6144), 1) + step * 6144
    good = lane < PAIRS * 384
    for k in range(SLOTS):
        if k < 5:
            v = x_ref[8 * k:8 * k + 8, :].astype(F32)
        else:
            v = jnp.concatenate([x_ref[40:45, :].astype(F32), jnp.zeros((3, 6144), F32)], 0)
        v = jnp.where(good, v, 0.0)
        for lp in range(16):
            for t in range(3):
                s_ref[3 * k + t, pl.ds(lp, 8, stride=17), :] = v[:, (3 * lp + t) * 128:(3 * lp + t + 1) * 128]
    rows = pl.ds(pl.multiple_of(16 * step, 16), 16)
    for a in range(NA):
        for q in range(18):
            o_ref[a, rows, q * 128:(q + 1) * 128] = s_ref[q, 17 * a:17 * a + 16, :].astype(BF)


def prep(x):
    return pl.pallas_call(
        prep_body,
        grid=(6,),
        out_shape=pltpu.VMEM((NA, LP, 2304), BF),
        in_specs=[pl.BlockSpec((ROWS, 6144), lambda i: (0, i))],
        out_specs=VMEM,
        scratch_shapes=[pltpu.VMEM((18, 136, 128), F32)],
        compiler_params=params(),
        name="prep",
    )(x)


def post_body(r_ref, o_ref, s_ref):
    rows = pl.ds(pl.multiple_of(16 * pl.program_id(0), 16), 16)
    for a in range(NA):
        for q in range(18):
            s_ref[q, 17 * a:17 * a + 16, :] = r_ref[a, rows, q * 128:(q + 1) * 128].astype(F32)
    for k in range(SLOTS):
        for lp in range(16):
            for t in range(3):
                v = s_ref[3 * k + t, pl.ds(lp, 8, stride=17), :].astype(BF)
                n = 8 if k < 5 else 5
                o_ref[8 * k:8 * k + n, (3 * lp + t) * 128:(3 * lp + t + 1) * 128] = v[:n]


def post(r):
    return pl.pallas_call(
        post_body,
        grid=(6,),
        out_shape=jax.ShapeDtypeStruct((ROWS, LON // NA * C), BF),
        in_specs=[VMEM],
        out_specs=pl.BlockSpec((ROWS, 6144), lambda i: (0, i)),
        scratch_shapes=[pltpu.VMEM((18, 136, 128), F32)],
        compiler_params=params(),
        name="post",
    )(near(r))


def whole(body, out, *args, scratch=(), name=None, far=False):
    return pl.pallas_call(
        body,
        in_specs=[VMEM] * len(args),
        out_specs=VMEM,
        out_shape=jax.ShapeDtypeStruct(out, BF) if far else pltpu.VMEM(out, BF),
        scratch_shapes=list(scratch),
        compiler_params=params(),
        name=name,
    )(*[near(a) for a in args])


def dft_f_body(r_ref, b_ref, g_ref, o_ref, x_ref):
    for k in range(SLOTS):
        v = r_ref[:, :, 384 * k:384 * k + 384].reshape(NA * LP, 384)
        x_ref[0:768, C * k:C * k + C] = v[:, :C]
        x_ref[768:1536, C * k:C * k + C] = v[:, C:]
    o_ref[:, 4:, :] = g_ref[...]
    y = dot(b_ref[...], x_ref[...], 1, 0).astype(BF)
    o_ref[:, :4, :] = y.reshape(128, 4, W)


def dft_f(r, bpt, wire_g):
    return whole(dft_f_body, (128, 8, W), r, bpt, wire_g, scratch=[pltpu.VMEM((1536, W), BF)], name="dft_f")


def dft_g_body(x_ref, b_ref, o_ref):
    y = dot(b_ref[...], x_ref[...], 1, 1).astype(BF)
    y = jnp.concatenate([y, jnp.zeros((512, W - 1080), BF)], 1)
    o_ref[...] = y.reshape(128, 4, W)


def dft_g(x, bdt):
    return whole(dft_g_body, (128, 4, W), x, bdt, name="dft_g")


def leg_body(r_ref, pf_ref, pi_ref, o_ref, s_ref, t_ref):
    for m in range(2):
        for r in range(2):
            v = r_ref[:, 2 * m + r, :]
            for k in range(SLOTS):
                s_ref[m, 128 * k:128 * k + 128, C * r:C * r + C] = v[:, C * k:C * k + C]
            v = r_ref[:, 4 + 2 * m + r, :].astype(F32).reshape(NP, NA, W)
            for a in range(NA):
                va = v[:, a, :].astype(BF)
                for t in range(48):
                    t_ref[m, 16 * t:16 * t + 16, C * r + 24 * a:C * r + 24 * a + 24] = va[:, 24 * t:24 * t + 24]
        o_ref[:, 384 * m:384 * m + 384] = dot(pf_ref[m], s_ref[m], 0, 0).astype(BF)
        o_ref[:, 768 + 384 * m:768 + 384 * m + 384] = dot(pi_ref[m], t_ref[m], 0, 0).astype(BF)


def leg(r, pf, pi):
    return whole(leg_body, (DEG, 1536), r, pf, pi, scratch=[pltpu.VMEM((2, 768, 384), BF)] * 2, name="leg")


def mix_body(r_ref, k_ref, o_ref, s_ref):
    i = lax.broadcasted_iota(jnp.int32, (256, 256), 0)
    j = lax.broadcasted_iota(jnp.int32, (256, 256), 1)
    perm = ((i // 16 == j % 16) & (i % 16 == j // 16)).astype(F32).astype(BF)
    x = dot(perm, r_ref[...].reshape(256, 1536), 1, 0).astype(BF)
    for l in range(16):
        for side in range(2):
            v = x[16 * l:16 * l + 16, 768 * side:768 * side + 768]
            v = jnp.concatenate([v[:, :384], v[:, 384:]], 0)
            y = dot(v, k_ref[l], 1, side).astype(BF)
            s_ref[16 * l:16 * l + 16, 768 * side:768 * side + 384] = y[:16]
            s_ref[16 * l:16 * l + 16, 768 * side + 384:768 * side + 768] = y[16:]
    o_ref[...] = dot(perm, s_ref[...], 1, 0).astype(BF).reshape(16, 16, 1536)


def mix(r, k):
    return whole(mix_body, (16, 16, 1536), r, k, scratch=[pltpu.VMEM((256, 1536), BF)], name="mix")


def syn_body(x_ref, pf_ref, pi_ref, o_ref, z_ref, y_ref):
    for m in range(2):
        y = dot(pi_ref[m], x_ref[:, 384 * m:384 * m + 384], 1, 0).astype(BF)
        for r in range(2):
            for a in range(NA):
                for t in range(48):
                    z_ref[a, :, 24 * t:24 * t + 24] = y[16 * t:16 * t + 16, C * r + 24 * a:C * r + 24 * a + 24]
            for p in range(NP):
                o_ref[8 * p:8 * p + 8, 2 * m + r, :] = z_ref[:, p, :]
        y = dot(pf_ref[m], x_ref[:, 768 + 384 * m:768 + 384 * m + 384], 1, 0).astype(BF)
        for r in range(2):
            for k in range(SLOTS):
                y_ref[:, C * k:C * k + C] = y[128 * k:128 * k + 128, C * r:C * r + C]
            o_ref[:, 4 + 2 * m + r, :] = y_ref[...]


def syn(x, pf, pi):
    return whole(syn_body, (128, 8, W), x, pf, pi, scratch=[pltpu.VMEM((8, 16, W), BF), pltpu.VMEM((128, W), BF)], name="syn")


def idft_f_body(y_ref, b_ref, o_ref):
    y = y_ref[:, :4, :].reshape(512, W)
    o_ref[...] = dot(y[:, :1080], b_ref[...], 0, 0).astype(BF)


def idft_f(y, bdt):
    return whole(idft_f_body, (1080, LON), y, bdt, name="idft_f", far=True)


def idft_g_body(y_ref, b_ref, o_ref):
    y = y_ref[:, 4:, :].reshape(512, W)
    z = dot(b_ref[...], y, 1, 0).astype(BF)
    for k in range(SLOTS):
        e = z[:768, C * k:C * k + C].reshape(NA, LP, C)
        o = z[768:, C * k:C * k + C].reshape(NA, LP, C)
        o_ref[:, :, 384 * k:384 * k + 384] = jnp.concatenate([e, o], 2)


def idft_g(y, bp):
    return whole(idft_g_body, (NA, LP, 2304), y, bp, name="idft_g")


def order_tables(table, first):
    part = lax.dynamic_slice(table, (0, first, 0), (LAT, 2, DEG))
    part = part.reshape(NP, ROWS, 2, DEG).transpose(2, 0, 1, 3)
    return jnp.pad(part, ((0, 0), (0, 0), (0, 3), (0, 0)))


def fence(*values):
    return lax.optimization_barrier(values)


def on_device(grid_input, cotangent, forward_legendre, inverse_legendre, filter_weight):
    bdt, bpt, bp = [jnp.asarray(t) for t in tables()]
    both = ("polar", "azimuth")
    first = 2 * lax.axis_index("azimuth")

    def over_all(x):
        return lax.all_to_all(x, both, 0, 0)

    def over_polar(x):
        return lax.all_to_all(x, "polar", 0, 0)

    def over_azimuth(x):
        return lax.all_to_all(x, "azimuth", 0, 0)

    spread = prep(grid_input)
    cot = cotangent.reshape(1080, LON)
    spread, cot = fence(spread, cot)
    got = over_azimuth(spread)
    wire_g = dft_g(cot, bdt)

    pf = order_tables(forward_legendre, first)
    pf = pf.reshape(2, NP, SLOTS, NA, DEG).transpose(0, 2, 1, 3, 4).reshape(2, 768, DEG)
    pi = order_tables(inverse_legendre, first)
    pi = pi.transpose(0, 2, 1, 3).reshape(2, 768, DEG)
    cube = filter_weight.reshape(16, 2, C, C)
    upper = jnp.concatenate([cube[:, 0], cube[:, 1]], axis=2)
    lower = jnp.concatenate([-cube[:, 1], cube[:, 0]], axis=2)
    kernel = jnp.concatenate([upper, lower], axis=1)

    got, wire_g, pf, pi, kernel = fence(got, wire_g, pf, pi, kernel)
    modes = leg(over_all(dft_f(got, bpt, wire_g)), pf, pi)
    modes = over_polar(modes.reshape(16, 16, 1536))
    modes = over_polar(mix(modes, kernel)).reshape(DEG, 1536)
    back = over_all(syn(modes, pf, pi))
    grad = over_azimuth(idft_g(back, bp))
    filtered = idft_f(back, bdt)
    filtered, grad = fence(filtered, grad)
    return filtered.reshape(ROWS, 24, LON), post(grad)


def solution(mesh):
    return jax.shard_map(
        on_device,
        mesh=mesh,
        in_specs=(
            P("polar", "azimuth"),
            P("polar", "azimuth", None),
            P(None, "polar", None),
            P(None, "polar", None),
            P("polar", None),
        ),
        out_specs=(P("polar", "azimuth", None), P("polar", "azimuth")),
        check_vma=False,
    )
```

```python
import functools
import math
import numpy as np
import ml_dtypes
import jax
import jax.numpy as jnp
from jax import lax
from jax.sharding import PartitionSpec as P
from jax.experimental import pallas as pl
from jax.experimental.pallas import tpu as pltpu

LAT = 720
LON = 1440
C = 192
DEG = 256
ORD = 256
NP = 16
NA = 8
ROWS = 45
SLOTS = 6
PAIRS = 90
LP = 96
W = 1152
F32 = jnp.float32
BF = jnp.bfloat16


def params():
    return pltpu.CompilerParams(vmem_limit_bytes=16 << 20)


def dot(a, b, ca, cb):
    return lax.dot_general(a, b, (((ca,), (cb,)), ((), ())), preferred_element_type=F32)


def tables():
    lon = np.arange(LON)[:, None]
    m = np.arange(ORD)[None, :]
    ang = ((lon * m) % LON) * (2.0 * math.pi / LON)
    fac = 1.0 / math.sqrt(LON)
    st = np.stack([np.cos(ang) * fac, -np.sin(ang) * fac], axis=-1).astype(np.float32)
    dbl = np.where(np.arange(ORD) == 0, 1.0, 2.0).astype(np.float32)[None, :, None]
    plain = st.reshape(LON, 2 * ORD).astype(ml_dtypes.bfloat16)
    doubled = (st * dbl).reshape(LON, 2 * ORD).astype(ml_dtypes.bfloat16)
    p4 = plain.reshape(NA, PAIRS, 2, 2 * ORD).transpose(2, 0, 1, 3)
    pp = np.zeros((2, NA, LP, 2 * ORD), ml_dtypes.bfloat16)
    pp[:, :, :PAIRS] = p4
    pp = pp.reshape(2 * NA * LP, 2 * ORD)
    return np.ascontiguousarray(doubled.T), np.ascontiguousarray(pp.T), pp


SMEM = pl.BlockSpec(memory_space=pltpu.SMEM)
VMEM = pl.BlockSpec(memory_space=pltpu.VMEM)


def near(x):
    return pltpu.with_memory_space_constraint(x, pltpu.VMEM)


def prep_body(x_ref, o_ref, s_ref):
    step = pl.program_id(0)
    lane = lax.broadcasted_iota(jnp.int32, (8, 6144), 1) + step * 6144
    good = lane < PAIRS * 384
    for k in range(SLOTS):
        if k < 5:
            v = x_ref[8 * k:8 * k + 8, :].astype(F32)
        else:
            v = jnp.concatenate([x_ref[40:45, :].astype(F32), jnp.zeros((3, 6144), F32)], 0)
        v = jnp.where(good, v, 0.0)
        for lp in range(16):
            for t in range(3):
                s_ref[3 * k + t, pl.ds(lp, 8, stride=17), :] = v[:, (3 * lp + t) * 128:(3 * lp + t + 1) * 128]
    rows = pl.ds(pl.multiple_of(16 * step, 16), 16)
    for a in range(NA):
        for q in range(18):
            o_ref[a, rows, q * 128:(q + 1) * 128] = s_ref[q, 17 * a:17 * a + 16, :].astype(BF)


def prep(x):
    return pl.pallas_call(
        prep_body,
        grid=(6,),
        out_shape=pltpu.VMEM((NA, LP, 2304), BF),
        in_specs=[pl.BlockSpec((ROWS, 6144), lambda i: (0, i))],
        out_specs=VMEM,
        scratch_shapes=[pltpu.VMEM((18, 136, 128), F32)],
        compiler_params=params(),
        name="prep",
    )(x)


def post_body(r_ref, o_ref, s_ref):
    rows = pl.ds(pl.multiple_of(16 * pl.program_id(0), 16), 16)
    for a in range(NA):
        for q in range(18):
            s_ref[q, 17 * a:17 * a + 16, :] = r_ref[a, rows, q * 128:(q + 1) * 128].astype(F32)
    for k in range(SLOTS):
        for lp in range(16):
            for t in range(3):
                v = s_ref[3 * k + t, pl.ds(lp, 8, stride=17), :].astype(BF)
                n = 8 if k < 5 else 5
                o_ref[8 * k:8 * k + n, (3 * lp + t) * 128:(3 * lp + t + 1) * 128] = v[:n]


def post(r):
    return pl.pallas_call(
        post_body,
        grid=(6,),
        out_shape=jax.ShapeDtypeStruct((ROWS, LON // NA * C), BF),
        in_specs=[VMEM],
        out_specs=pl.BlockSpec((ROWS, 6144), lambda i: (0, i)),
        scratch_shapes=[pltpu.VMEM((18, 136, 128), F32)],
        compiler_params=params(),
        name="post",
    )(near(r))


def whole(body, out, *args, scratch=(), name=None, far=False):
    return pl.pallas_call(
        body,
        in_specs=[VMEM] * len(args),
        out_specs=VMEM,
        out_shape=jax.ShapeDtypeStruct(out, BF) if far else pltpu.VMEM(out, BF),
        scratch_shapes=list(scratch),
        compiler_params=params(),
        name=name,
    )(*[near(a) for a in args])


def dft_f_body(r_ref, b_ref, g_ref, o_ref, x_ref):
    for k in range(SLOTS):
        v = r_ref[:, :, 384 * k:384 * k + 384].reshape(NA * LP, 384)
        x_ref[0:768, C * k:C * k + C] = v[:, :C]
        x_ref[768:1536, C * k:C * k + C] = v[:, C:]
    o_ref[:, 4:, :] = g_ref[...]
    y = dot(b_ref[...], x_ref[...], 1, 0).astype(BF)
    o_ref[:, :4, :] = y.reshape(128, 4, W)


def dft_f(r, bpt, wire_g):
    return whole(dft_f_body, (128, 8, W), r, bpt, wire_g, scratch=[pltpu.VMEM((1536, W), BF)], name="dft_f")


def dft_g_body(x_ref, b_ref, o_ref):
    y = dot(b_ref[...], x_ref[...], 1, 1).astype(BF)
    y = jnp.concatenate([y, jnp.zeros((512, W - 1080), BF)], 1)
    o_ref[...] = y.reshape(128, 4, W)


def dft_g(x, bdt):
    return whole(dft_g_body, (128, 4, W), x, bdt, name="dft_g")


def swap_rows(x, rows, cols):
    n = rows * cols
    i = lax.broadcasted_iota(jnp.int32, (n, n), 0)
    j = lax.broadcasted_iota(jnp.int32, (n, n), 1)
    perm = ((i // rows == j % cols) & (i % rows == j // cols)).astype(F32).astype(BF)
    return dot(perm, x, 1, 0).astype(BF)


def leg_body(r_ref, pf_ref, pi_ref, o_ref, s_ref, t_ref):
    for a in range(NA):
        v = swap_rows(r_ref[:, a, :, :].reshape(128, W), NP, 8)
        for j in range(4):
            m, r = j // 2, j % 2
            for k in range(SLOTS):
                row = 128 * k + 16 * a
                s_ref[m, row:row + 16, C * r:C * r + C] = v[16 * j:16 * j + 16, C * k:C * k + C]
            for t in range(48):
                lane = C * r + 24 * a
                t_ref[m, 16 * t:16 * t + 16, lane:lane + 24] = v[64 + 16 * j:80 + 16 * j, 24 * t:24 * t + 24]
    for m in range(2):
        o_ref[:, 384 * m:384 * m + 384] = dot(pf_ref[m], s_ref[m], 0, 0).astype(BF)
        o_ref[:, 768 + 384 * m:768 + 384 * m + 384] = dot(pi_ref[m], t_ref[m], 0, 0).astype(BF)


def leg(r, pf, pi):
    r = r.reshape(NP, NA, 8, W)
    return whole(leg_body, (DEG, 1536), r, pf, pi, scratch=[pltpu.VMEM((2, 768, 384), BF)] * 2, name="leg")


def mix_body(r_ref, k_ref, o_ref, s_ref):
    i = lax.broadcasted_iota(jnp.int32, (256, 256), 0)
    j = lax.broadcasted_iota(jnp.int32, (256, 256), 1)
    perm = ((i // 16 == j % 16) & (i % 16 == j // 16)).astype(F32).astype(BF)
    x = dot(perm, r_ref[...].reshape(256, 1536), 1, 0).astype(BF)
    for l in range(16):
        for side in range(2):
            v = x[16 * l:16 * l + 16, 768 * side:768 * side + 768]
            v = jnp.concatenate([v[:, :384], v[:, 384:]], 0)
            y = dot(v, k_ref[l], 1, side).astype(BF)
            s_ref[16 * l:16 * l + 16, 768 * side:768 * side + 384] = y[:16]
            s_ref[16 * l:16 * l + 16, 768 * side + 384:768 * side + 768] = y[16:]
    o_ref[...] = dot(perm, s_ref[...], 1, 0).astype(BF).reshape(16, 16, 1536)


def mix(r, k):
    return whole(mix_body, (16, 16, 1536), r, k, scratch=[pltpu.VMEM((256, 1536), BF)], name="mix")


def syn_body(x_ref, pf_ref, pi_ref, o_ref, y_ref, z_ref):
    for m in range(2):
        y_ref[m] = dot(pi_ref[m], x_ref[:, 384 * m:384 * m + 384], 1, 0).astype(BF)
        y_ref[2 + m] = dot(pf_ref[m], x_ref[:, 768 + 384 * m:768 + 384 * m + 384], 1, 0).astype(BF)
    for a in range(NA):
        for j in range(4):
            m, r = j // 2, j % 2
            for t in range(48):
                lane = C * r + 24 * a
                z_ref[16 * j:16 * j + 16, 24 * t:24 * t + 24] = y_ref[m, 16 * t:16 * t + 16, lane:lane + 24]
            for k in range(SLOTS):
                row = 128 * k + 16 * a
                z_ref[64 + 16 * j:80 + 16 * j, C * k:C * k + C] = y_ref[2 + m, row:row + 16, C * r:C * r + C]
        o_ref[:, a, :, :] = swap_rows(z_ref[...], 8, NP).reshape(NP, 8, W)


def syn(x, pf, pi):
    scratch = [pltpu.VMEM((4, 768, 384), BF), pltpu.VMEM((128, W), BF)]
    return whole(syn_body, (NP, NA, 8, W), x, pf, pi, scratch=scratch, name="syn").reshape(128, 8, W)


def idft_f_body(y_ref, b_ref, o_ref):
    y = y_ref[:, :4, :].reshape(512, W)
    o_ref[...] = dot(y[:, :1080], b_ref[...], 0, 0).astype(BF)


def idft_f(y, bdt):
    return whole(idft_f_body, (1080, LON), y, bdt, name="idft_f", far=True)


def idft_g_body(y_ref, b_ref, o_ref):
    y = y_ref[:, 4:, :].reshape(512, W)
    z = dot(b_ref[...], y, 1, 0).astype(BF)
    for k in range(SLOTS):
        e = z[:768, C * k:C * k + C].reshape(NA, LP, C)
        o = z[768:, C * k:C * k + C].reshape(NA, LP, C)
        o_ref[:, :, 384 * k:384 * k + 384] = jnp.concatenate([e, o], 2)


def idft_g(y, bp):
    return whole(idft_g_body, (NA, LP, 2304), y, bp, name="idft_g")


def order_tables(table, first):
    part = lax.dynamic_slice(table, (0, first, 0), (LAT, 2, DEG))
    part = part.reshape(NP, ROWS, 2, DEG).transpose(2, 1, 0, 3)
    return jnp.pad(part, ((0, 0), (0, 3), (0, 0), (0, 0))).reshape(2, 768, DEG)


def fence(*values):
    return lax.optimization_barrier(values)


def on_device(grid_input, cotangent, forward_legendre, inverse_legendre, filter_weight):
    bdt, bpt, bp = [jnp.asarray(t) for t in tables()]
    both = ("polar", "azimuth")
    first = 2 * lax.axis_index("azimuth")

    def over_all(x):
        return lax.all_to_all(x, both, 0, 0)

    def over_polar(x):
        return lax.all_to_all(x, "polar", 0, 0)

    def over_azimuth(x):
        return lax.all_to_all(x, "azimuth", 0, 0)

    spread = prep(grid_input)
    cot = cotangent.reshape(1080, LON)
    spread, cot = fence(spread, cot)
    got = over_azimuth(spread)
    wire_g = dft_g(cot, bdt)

    pf = order_tables(forward_legendre, first)
    pi = order_tables(inverse_legendre, first)
    cube = filter_weight.reshape(16, 2, C, C)
    upper = jnp.concatenate([cube[:, 0], cube[:, 1]], axis=2)
    lower = jnp.concatenate([-cube[:, 1], cube[:, 0]], axis=2)
    kernel = jnp.concatenate([upper, lower], axis=1)

    got, wire_g, pf, pi, kernel, bpt = fence(got, wire_g, pf, pi, kernel, bpt)
    modes = leg(over_all(dft_f(got, bpt, wire_g)), pf, pi)
    modes = over_polar(modes.reshape(16, 16, 1536))
    modes = over_polar(mix(modes, kernel)).reshape(DEG, 1536)
    back = over_all(syn(modes, pf, pi))
    grad = over_azimuth(idft_g(back, bp))
    filtered = idft_f(back, bdt)
    filtered, grad = fence(filtered, grad)
    return filtered.reshape(ROWS, 24, LON), post(grad)


def solution(mesh):
    return jax.shard_map(
        on_device,
        mesh=mesh,
        in_specs=(
            P("polar", "azimuth"),
            P("polar", "azimuth", None),
            P(None, "polar", None),
            P(None, "polar", None),
            P("polar", None),
        ),
        out_specs=(P("polar", "azimuth", None), P("polar", "azimuth")),
        check_vma=False,
    )
```

```python
import functools
import math
import numpy as np
import ml_dtypes
import jax
import jax.numpy as jnp
from jax import lax
from jax.sharding import PartitionSpec as P
from jax.experimental import pallas as pl
from jax.experimental.pallas import tpu as pltpu

LAT = 720
LON = 1440
C = 192
DEG = 256
ORD = 256
NP = 16
NA = 8
ROWS = 45
SLOTS = 6
PAIRS = 90
LP = 96
W = 1152
F32 = jnp.float32
BF = jnp.bfloat16


def params():
    return pltpu.CompilerParams(vmem_limit_bytes=20 << 20)


def dot(a, b, ca, cb):
    return lax.dot_general(a, b, (((ca,), (cb,)), ((), ())), preferred_element_type=F32)


def tables():
    lon = np.arange(LON)[:, None]
    m = np.arange(ORD)[None, :]
    ang = ((lon * m) % LON) * (2.0 * math.pi / LON)
    fac = 1.0 / math.sqrt(LON)
    st = np.stack([np.cos(ang) * fac, -np.sin(ang) * fac], axis=-1).astype(np.float32)
    dbl = np.where(np.arange(ORD) == 0, 1.0, 2.0).astype(np.float32)[None, :, None]
    plain = st.reshape(LON, 2 * ORD).astype(ml_dtypes.bfloat16)
    doubled = (st * dbl).reshape(LON, 2 * ORD).astype(ml_dtypes.bfloat16)
    p4 = plain.reshape(NA, PAIRS, 2, 2 * ORD).transpose(0, 2, 1, 3)
    pp = np.zeros((NA, 2, LP, 2 * ORD), ml_dtypes.bfloat16)
    pp[:, :, :PAIRS] = p4
    pp = pp.reshape(2 * NA * LP, 2 * ORD)
    return np.ascontiguousarray(doubled.T), np.ascontiguousarray(pp.T), pp


SMEM = pl.BlockSpec(memory_space=pltpu.SMEM)
VMEM = pl.BlockSpec(memory_space=pltpu.VMEM)


ANY = pl.BlockSpec(memory_space=pl.ANY)


def away(x):
    return pltpu.with_memory_space_constraint(x, pltpu.HBM)


def near(x):
    return pltpu.with_memory_space_constraint(x, pltpu.VMEM)


CHUNKS = [(6144 * i, min(6144, PAIRS * 384 - 6144 * i)) for i in range(6)]


def prep_body(x_hbm, o_hbm, x_ref, y_ref, s_ref, in_sem, out_sem):
    loads = []
    for i, (lane, n) in enumerate(CHUNKS):
        part = pl.ds(lane, n)
        loads.append(pltpu.make_async_copy(x_hbm.at[:, part], x_ref.at[:, part], in_sem.at[i]))
        loads[i].start()
    stores = []
    for i, (lane, n) in enumerate(CHUNKS):
        loads[i].wait()
        for k in range(SLOTS):
            if k < 5:
                v = x_ref[8 * k:8 * k + 8, lane:lane + n].astype(F32)
            else:
                v = jnp.concatenate([x_ref[40:45, lane:lane + n].astype(F32), jnp.zeros((3, n), F32)], 0)
            for lp in range(16):
                for t in range(3):
                    at = (3 * lp + t) * 128
                    w = v[:, at:at + 128] if at < n else jnp.zeros((8, 128), F32)
                    s_ref[3 * k + t, pl.ds(lp, 8, stride=17), :] = w
        for a in range(NA):
            for q in range(18):
                y_ref[a, 16 * i:16 * i + 16, q * 128:(q + 1) * 128] = s_ref[q, 17 * a:17 * a + 16, :].astype(BF)
        part = pl.ds(16 * i, 16)
        stores.append(pltpu.make_async_copy(y_ref.at[:, part, :], o_hbm.at[:, part, :], out_sem.at[i]))
        stores[i].start()
    for copy in stores:
        copy.wait()


def prep(x):
    return pl.pallas_call(
        prep_body,
        in_specs=[ANY],
        out_specs=ANY,
        out_shape=pltpu.HBM((NA, LP, 2304), BF),
        scratch_shapes=[
            pltpu.VMEM((ROWS, PAIRS * 384), BF),
            pltpu.VMEM((NA, LP, 2304), BF),
            pltpu.VMEM((18, 136, 128), F32),
            pltpu.SemaphoreType.DMA((6,)),
            pltpu.SemaphoreType.DMA((6,)),
        ],
        compiler_params=params(),
        name="prep",
    )(away(x))


def post_body(r_hbm, o_hbm, r_ref, y_ref, s_ref, in_sem, out_sem):
    loads = []
    for i in range(6):
        part = pl.ds(16 * i, 16)
        loads.append(pltpu.make_async_copy(r_hbm.at[:, part, :], r_ref.at[:, part, :], in_sem.at[i]))
        loads[i].start()
    stores = []
    for i, (lane, n) in enumerate(CHUNKS):
        loads[i].wait()
        for a in range(NA):
            for q in range(18):
                s_ref[q, 17 * a:17 * a + 16, :] = r_ref[a, 16 * i:16 * i + 16, q * 128:(q + 1) * 128].astype(F32)
        for k in range(SLOTS):
            for lp in range(n // 384):
                for t in range(3):
                    v = s_ref[3 * k + t, pl.ds(lp, 8, stride=17), :].astype(BF)
                    c = 8 if k < 5 else 5
                    at = lane + (3 * lp + t) * 128
                    y_ref[8 * k:8 * k + c, at:at + 128] = v[:c]
        part = pl.ds(lane, n)
        stores.append(pltpu.make_async_copy(y_ref.at[:, part], o_hbm.at[:, part], out_sem.at[i]))
        stores[i].start()
    for copy in stores:
        copy.wait()


def post(r):
    return pl.pallas_call(
        post_body,
        in_specs=[ANY],
        out_specs=ANY,
        out_shape=pltpu.HBM((ROWS, PAIRS * 384), BF),
        scratch_shapes=[
            pltpu.VMEM((NA, LP, 2304), BF),
            pltpu.VMEM((ROWS, PAIRS * 384), BF),
            pltpu.VMEM((18, 136, 128), F32),
            pltpu.SemaphoreType.DMA((6,)),
            pltpu.SemaphoreType.DMA((6,)),
        ],
        compiler_params=params(),
        name="post",
    )(away(r))


def whole(body, out, *args, scratch=(), name=None, far=False):
    return pl.pallas_call(
        body,
        in_specs=[VMEM] * len(args),
        out_specs=VMEM,
        out_shape=jax.ShapeDtypeStruct(out, BF) if far else pltpu.VMEM(out, BF),
        scratch_shapes=list(scratch),
        compiler_params=params(),
        name=name,
    )(*[near(a) for a in args])


def dft_f_body(r_ref, b_hbm, g_hbm, o_ref, x_ref, b_ref, g_ref, sem):
    load_b = pltpu.make_async_copy(b_hbm, b_ref, sem.at[0])
    load_g = pltpu.make_async_copy(g_hbm, g_ref, sem.at[1])
    load_b.start()
    load_g.start()
    for blk in range(NA):
        for k in range(SLOTS):
            v = r_ref[blk, :, 384 * k:384 * k + 384]
            row = 2 * LP * blk
            x_ref[row:row + LP, C * k:C * k + C] = v[:, :C]
            x_ref[row + LP:row + 2 * LP, C * k:C * k + C] = v[:, C:]
    load_b.wait()
    y = dot(b_ref[...], x_ref[...], 1, 0).astype(BF)
    load_g.wait()
    o_ref[:, 4:, :] = g_ref[...]
    o_ref[:, :4, :] = y.reshape(128, 4, W)


def dft_f(r, bpt, wire_g):
    return pl.pallas_call(
        dft_f_body,
        in_specs=[VMEM, ANY, ANY],
        out_specs=VMEM,
        out_shape=pltpu.VMEM((128, 8, W), BF),
        scratch_shapes=[
            pltpu.VMEM((1536, W), BF),
            pltpu.VMEM((512, 1536), BF),
            pltpu.VMEM((128, 4, W), BF),
            pltpu.SemaphoreType.DMA((2,)),
        ],
        compiler_params=params(),
        name="dft_f",
    )(near(r), away(bpt), away(wire_g))


def dft_g_body(x_ref, b_ref, o_ref):
    y = dot(b_ref[...], x_ref[...], 1, 1).astype(BF)
    y = jnp.concatenate([y, jnp.zeros((512, W - 1080), BF)], 1)
    o_ref[...] = y.reshape(128, 4, W)


def dft_g(x, bdt):
    return whole(dft_g_body, (128, 4, W), x, bdt, name="dft_g")


def swap_rows(x, rows, cols):
    n = rows * cols
    i = lax.broadcasted_iota(jnp.int32, (n, n), 0)
    j = lax.broadcasted_iota(jnp.int32, (n, n), 1)
    perm = ((i // rows == j % cols) & (i % rows == j // cols)).astype(F32).astype(BF)
    return dot(perm, x, 1, 0).astype(BF)


def leg_body(r_ref, pf_ref, pi_ref, o_ref, s_ref, t_ref):
    for a in range(NA):
        v = swap_rows(r_ref[:, a, :, :].reshape(128, W), NP, 8)
        for j in range(4):
            m, r = j // 2, j % 2
            for k in range(SLOTS):
                row = 128 * k + 16 * a
                s_ref[m, row:row + 16, C * r:C * r + C] = v[16 * j:16 * j + 16, C * k:C * k + C]
            for t in range(48):
                lane = C * r + 24 * a
                t_ref[m, 16 * t:16 * t + 16, lane:lane + 24] = v[64 + 16 * j:80 + 16 * j, 24 * t:24 * t + 24]
    for m in range(2):
        o_ref[:, 384 * m:384 * m + 384] = dot(pf_ref[m], s_ref[m], 0, 0).astype(BF)
        o_ref[:, 768 + 384 * m:768 + 384 * m + 384] = dot(pi_ref[m], t_ref[m], 0, 0).astype(BF)


def leg(r, pf, pi):
    r = r.reshape(NP, NA, 8, W)
    return whole(leg_body, (DEG, 1536), r, pf, pi, scratch=[pltpu.VMEM((2, 768, 384), BF)] * 2, name="leg")


def mix_body(r_ref, k_ref, o_ref, s_ref):
    i = lax.broadcasted_iota(jnp.int32, (256, 256), 0)
    j = lax.broadcasted_iota(jnp.int32, (256, 256), 1)
    perm = ((i // 16 == j % 16) & (i % 16 == j // 16)).astype(F32).astype(BF)
    x = dot(perm, r_ref[...].reshape(256, 1536), 1, 0).astype(BF)
    for l in range(16):
        for side in range(2):
            v = x[16 * l:16 * l + 16, 768 * side:768 * side + 768]
            v = jnp.concatenate([v[:, :384], v[:, 384:]], 0)
            y = dot(v, k_ref[l], 1, side).astype(BF)
            s_ref[16 * l:16 * l + 16, 768 * side:768 * side + 384] = y[:16]
            s_ref[16 * l:16 * l + 16, 768 * side + 384:768 * side + 768] = y[16:]
    o_ref[...] = dot(perm, s_ref[...], 1, 0).astype(BF).reshape(16, 16, 1536)


def mix(r, k):
    return whole(mix_body, (16, 16, 1536), r, k, scratch=[pltpu.VMEM((256, 1536), BF)], name="mix")


def syn_body(x_ref, pf_ref, pi_ref, o_ref, y_ref, z_ref):
    for m in range(2):
        y_ref[m] = dot(pi_ref[m], x_ref[:, 384 * m:384 * m + 384], 1, 0).astype(BF)
        y_ref[2 + m] = dot(pf_ref[m], x_ref[:, 768 + 384 * m:768 + 384 * m + 384], 1, 0).astype(BF)
    for a in range(NA):
        for j in range(4):
            m, r = j // 2, j % 2
            for t in range(48):
                lane = C * r + 24 * a
                z_ref[16 * j:16 * j + 16, 24 * t:24 * t + 24] = y_ref[m, 16 * t:16 * t + 16, lane:lane + 24]
            for k in range(SLOTS):
                row = 128 * k + 16 * a
                z_ref[64 + 16 * j:80 + 16 * j, C * k:C * k + C] = y_ref[2 + m, row:row + 16, C * r:C * r + C]
        o_ref[:, a, :, :] = swap_rows(z_ref[...], 8, NP).reshape(NP, 8, W)


def syn(x, pf, pi):
    scratch = [pltpu.VMEM((4, 768, 384), BF), pltpu.VMEM((128, W), BF)]
    return whole(syn_body, (NP, NA, 8, W), x, pf, pi, scratch=scratch, name="syn").reshape(128, 8, W)


def idft_f_body(y_ref, b_ref, o_ref):
    y = y_ref[:, :4, :].reshape(512, W)
    o_ref[...] = dot(y[:, :1080], b_ref[...], 0, 0).astype(BF)


def idft_f(y, bdt):
    return whole(idft_f_body, (1080, LON), y, bdt, name="idft_f", far=True)


def idft_g_body(y_ref, b_ref, o_hbm, o_ref, sem):
    y = y_ref[:, 4:, :].reshape(512, W)
    stores = []
    for i in range(4):
        z = dot(b_ref[4 * LP * i:4 * LP * (i + 1), :], y, 1, 0).astype(BF)
        for half in range(2):
            row = 2 * LP * half
            for k in range(SLOTS):
                e = z[row:row + LP, C * k:C * k + C]
                o = z[row + LP:row + 2 * LP, C * k:C * k + C]
                o_ref[2 * i + half, :, 384 * k:384 * k + 384] = jnp.concatenate([e, o], 1)
        part = pl.ds(2 * i, 2)
        stores.append(pltpu.make_async_copy(o_ref.at[part], o_hbm.at[part], sem.at[i]))
        stores[i].start()
    for copy in stores:
        copy.wait()


def idft_g(y, bp):
    return pl.pallas_call(
        idft_g_body,
        in_specs=[VMEM, VMEM],
        out_specs=ANY,
        out_shape=pltpu.HBM((NA, LP, 2304), BF),
        scratch_shapes=[pltpu.VMEM((NA, LP, 2304), BF), pltpu.SemaphoreType.DMA((4,))],
        compiler_params=params(),
        name="idft_g",
    )(near(y), near(bp))


def order_tables(table, first):
    part = lax.dynamic_slice(table, (0, first, 0), (LAT, 2, DEG))
    part = part.reshape(NP, ROWS, 2, DEG).transpose(2, 1, 0, 3)
    return jnp.pad(part, ((0, 0), (0, 3), (0, 0), (0, 0))).reshape(2, 768, DEG)


def fence(*values):
    return lax.optimization_barrier(values)


def on_device(grid_input, cotangent, forward_legendre, inverse_legendre, filter_weight):
    bdt, bpt, bp = [jnp.asarray(t) for t in tables()]
    both = ("polar", "azimuth")
    first = 2 * lax.axis_index("azimuth")

    def over_all(x):
        return lax.all_to_all(x, both, 0, 0)

    def over_polar(x):
        return lax.all_to_all(x, "polar", 0, 0)

    def over_azimuth(x):
        return lax.all_to_all(x, "azimuth", 0, 0)

    spread = prep(grid_input)
    cot = cotangent.reshape(1080, LON)
    spread, cot = fence(spread, cot)
    got = over_azimuth(spread)
    wire_g = dft_g(cot, bdt)

    pf = order_tables(forward_legendre, first)
    pi = order_tables(inverse_legendre, first)
    cube = filter_weight.reshape(16, 2, C, C)
    upper = jnp.concatenate([cube[:, 0], cube[:, 1]], axis=2)
    lower = jnp.concatenate([-cube[:, 1], cube[:, 0]], axis=2)
    kernel = jnp.concatenate([upper, lower], axis=1)

    got, wire_g, pf, pi, kernel = fence(got, wire_g, pf, pi, kernel)
    modes = leg(over_all(dft_f(got, bpt, wire_g)), pf, pi)
    modes = over_polar(modes.reshape(16, 16, 1536))
    modes = over_polar(mix(modes, kernel)).reshape(DEG, 1536)
    back = over_all(syn(modes, pf, pi))
    grad = over_azimuth(idft_g(back, bp))
    filtered = idft_f(back, bdt)
    filtered, grad = fence(filtered, grad)
    return filtered.reshape(ROWS, 24, LON), post(grad)


def solution(mesh):
    return jax.shard_map(
        on_device,
        mesh=mesh,
        in_specs=(
            P("polar", "azimuth"),
            P("polar", "azimuth", None),
            P(None, "polar", None),
            P(None, "polar", None),
            P("polar", None),
        ),
        out_specs=(P("polar", "azimuth", None), P("polar", "azimuth")),
        check_vma=False,
    )
```

```python
import functools
import math
import numpy as np
import ml_dtypes
import jax
import jax.numpy as jnp
from jax import lax
from jax.sharding import PartitionSpec as P
from jax.experimental import pallas as pl
from jax.experimental.pallas import tpu as pltpu

LAT = 720
LON = 1440
C = 192
DEG = 256
ORD = 256
NP = 16
NA = 8
ROWS = 45
SLOTS = 6
PAIRS = 90
LP = 96
W = 1152
F32 = jnp.float32
BF = jnp.bfloat16


def params():
    return pltpu.CompilerParams(vmem_limit_bytes=20 << 20)


def dot(a, b, ca, cb):
    return lax.dot_general(a, b, (((ca,), (cb,)), ((), ())), preferred_element_type=F32)


def tables():
    lon = np.arange(LON)[:, None]
    m = np.arange(ORD)[None, :]
    ang = ((lon * m) % LON) * (2.0 * math.pi / LON)
    fac = 1.0 / math.sqrt(LON)
    st = np.stack([np.cos(ang) * fac, -np.sin(ang) * fac], axis=-1).astype(np.float32)
    dbl = np.where(np.arange(ORD) == 0, 1.0, 2.0).astype(np.float32)[None, :, None]
    plain = st.reshape(LON, 2 * ORD).astype(ml_dtypes.bfloat16)
    doubled = (st * dbl).reshape(LON, 2 * ORD).astype(ml_dtypes.bfloat16)
    p4 = plain.reshape(NA, PAIRS, 2, 2 * ORD).transpose(0, 2, 1, 3)
    pp = np.zeros((NA, 2, LP, 2 * ORD), ml_dtypes.bfloat16)
    pp[:, :, :PAIRS] = p4
    pp = pp.reshape(2 * NA * LP, 2 * ORD)
    return np.ascontiguousarray(doubled.T), np.ascontiguousarray(pp.T), pp


SMEM = pl.BlockSpec(memory_space=pltpu.SMEM)
VMEM = pl.BlockSpec(memory_space=pltpu.VMEM)


ANY = pl.BlockSpec(memory_space=pl.ANY)


def away(x):
    return pltpu.with_memory_space_constraint(x, pltpu.HBM)


def near(x):
    return pltpu.with_memory_space_constraint(x, pltpu.VMEM)


WIRE = 272 * SLOTS
STRIDE = 273


def slot_rows(k):
    return pl.ds(8 * k, 8 if k < 5 else 5)


def prep_body(x_hbm, o_hbm, x_ref, y_ref, s_ref, in_sem, out_sem):
    loads = []
    for k in range(SLOTS):
        rows = slot_rows(k)
        loads.append(pltpu.make_async_copy(x_hbm.at[rows, :], x_ref.at[rows, :], in_sem.at[k]))
        loads[k].start()
    stores = []
    for k in range(SLOTS):
        loads[k].wait()
        for g in range(6):
            lane, n = 5760 * g, 5760
            if k < 5:
                v = x_ref[8 * k:8 * k + 8, lane:lane + n].astype(F32)
            else:
                v = jnp.concatenate([x_ref[40:45, lane:lane + n].astype(F32), jnp.zeros((3, n), F32)], 0)
            for i in range(15):
                for t in range(3):
                    at = (3 * i + t) * 128
                    s_ref[pl.ds(90 * t + 15 * g + i, 8, stride=STRIDE), :] = v[:, at:at + 128]
        for a in range(NA):
            y_ref[a, 272 * k:272 * k + 272, :] = s_ref[STRIDE * a:STRIDE * a + 272, :].astype(BF)
        part = pl.ds(272 * k, 272)
        stores.append(pltpu.make_async_copy(y_ref.at[:, part, :], o_hbm.at[:, part, :], out_sem.at[k]))
        stores[k].start()
    for copy in stores:
        copy.wait()


def edge(body, out, x, name):
    return pl.pallas_call(
        body,
        in_specs=[ANY],
        out_specs=ANY,
        out_shape=pltpu.HBM(out, BF),
        scratch_shapes=[
            pltpu.VMEM(x.shape, BF),
            pltpu.VMEM(out, BF),
            pltpu.VMEM((STRIDE * NA, 128), F32),
            pltpu.SemaphoreType.DMA((SLOTS,)),
            pltpu.SemaphoreType.DMA((SLOTS,)),
        ],
        compiler_params=params(),
        name=name,
    )(away(x))


def prep(x):
    return edge(prep_body, (NA, WIRE, 128), x, "prep")


def post_body(r_hbm, o_hbm, r_ref, y_ref, s_ref, in_sem, out_sem):
    loads = []
    for k in range(SLOTS):
        part = pl.ds(272 * k, 272)
        loads.append(pltpu.make_async_copy(r_hbm.at[:, part, :], r_ref.at[:, part, :], in_sem.at[k]))
        loads[k].start()
    stores = []
    for k in range(SLOTS):
        loads[k].wait()
        for a in range(NA):
            s_ref[STRIDE * a:STRIDE * a + 272, :] = r_ref[a, 272 * k:272 * k + 272, :].astype(F32)
        c = 8 if k < 5 else 5
        for lp in range(PAIRS):
            for t in range(3):
                v = s_ref[pl.ds(90 * t + lp, 8, stride=STRIDE), :].astype(BF)
                at = (3 * lp + t) * 128
                y_ref[8 * k:8 * k + c, at:at + 128] = v[:c]
        rows = slot_rows(k)
        stores.append(pltpu.make_async_copy(y_ref.at[rows, :], o_hbm.at[rows, :], out_sem.at[k]))
        stores[k].start()
    for copy in stores:
        copy.wait()


def post(r):
    return edge(post_body, (ROWS, PAIRS * 384), r, "post")


def whole(body, out, *args, scratch=(), name=None, far=False):
    return pl.pallas_call(
        body,
        in_specs=[VMEM] * len(args),
        out_specs=VMEM,
        out_shape=jax.ShapeDtypeStruct(out, BF) if far else pltpu.VMEM(out, BF),
        scratch_shapes=list(scratch),
        compiler_params=params(),
        name=name,
    )(*[near(a) for a in args])


def dft_f_body(r_ref, b_hbm, g_hbm, o_ref, x_ref, w_ref, b_ref, g_ref, sem):
    load_b = pltpu.make_async_copy(b_hbm, b_ref, sem.at[0])
    load_g = pltpu.make_async_copy(g_hbm, g_ref, sem.at[1])
    load_b.start()
    load_g.start()

    def gather(to_ref, slots):
        for blk in range(NA):
            row = 2 * LP * blk
            for end in (row + LP, row + 2 * LP):
                to_ref[end - 16:end, :] = jnp.zeros((16, C * len(slots)), BF)
            for i, k in enumerate(slots):
                at = 272 * k
                v = [r_ref[blk, at + 90 * t:at + 90 * t + 90, :] for t in range(3)]
                to_ref[row:row + 90, C * i:C * i + C] = jnp.concatenate([v[0], v[1][:, :64]], 1)
                to_ref[row + LP:row + LP + 90, C * i:C * i + C] = jnp.concatenate([v[1][:, 64:], v[2]], 1)

    gather(x_ref, (0, 1, 2, 3))
    load_b.wait()
    y = dot(b_ref[...], x_ref[...], 1, 0).astype(BF)
    gather(w_ref, (4, 5))
    o_ref[:, :4, :768] = y.reshape(128, 4, 768)
    y = dot(b_ref[...], w_ref[...], 1, 0).astype(BF)
    load_g.wait()
    o_ref[:, 4:, :] = g_ref[...]
    o_ref[:, :4, 768:] = y.reshape(128, 4, 384)


def dft_f(r, bpt, wire_g):
    return pl.pallas_call(
        dft_f_body,
        in_specs=[VMEM, ANY, ANY],
        out_specs=VMEM,
        out_shape=pltpu.VMEM((128, 8, W), BF),
        scratch_shapes=[
            pltpu.VMEM((1536, 768), BF),
            pltpu.VMEM((1536, 384), BF),
            pltpu.VMEM((512, 1536), BF),
            pltpu.VMEM((128, 4, W), BF),
            pltpu.SemaphoreType.DMA((2,)),
        ],
        compiler_params=params(),
        name="dft_f",
    )(near(r), away(bpt), away(wire_g))


def dft_g_body(x_ref, b_ref, o_ref):
    y = dot(b_ref[...], x_ref[...], 1, 1).astype(BF)
    y = jnp.concatenate([y, jnp.zeros((512, W - 1080), BF)], 1)
    o_ref[...] = y.reshape(128, 4, W)


def dft_g(x, bdt):
    return whole(dft_g_body, (128, 4, W), x, bdt, name="dft_g")


def swap_rows(x, rows, cols):
    n = rows * cols
    i = lax.broadcasted_iota(jnp.int32, (n, n), 0)
    j = lax.broadcasted_iota(jnp.int32, (n, n), 1)
    perm = ((i // rows == j % cols) & (i % rows == j // cols)).astype(F32).astype(BF)
    return dot(perm, x, 1, 0).astype(BF)


def leg_body(r_ref, pf_ref, pi_ref, o_ref, s_ref, t_ref):
    for a in range(NA):
        v = swap_rows(r_ref[:, a, :, :].reshape(128, W), NP, 8)
        for j in range(4):
            m, r = j // 2, j % 2
            for k in range(SLOTS):
                row = 128 * k + 16 * a
                s_ref[m, row:row + 16, C * r:C * r + C] = v[16 * j:16 * j + 16, C * k:C * k + C]
            for t in range(48):
                lane = C * r + 24 * a
                t_ref[m, 16 * t:16 * t + 16, lane:lane + 24] = v[64 + 16 * j:80 + 16 * j, 24 * t:24 * t + 24]
    for m in range(2):
        o_ref[:, 384 * m:384 * m + 384] = dot(pf_ref[m], s_ref[m], 0, 0).astype(BF)
        o_ref[:, 768 + 384 * m:768 + 384 * m + 384] = dot(pi_ref[m], t_ref[m], 0, 0).astype(BF)


def leg(r, pf, pi):
    r = r.reshape(NP, NA, 8, W)
    return whole(leg_body, (DEG, 1536), r, pf, pi, scratch=[pltpu.VMEM((2, 768, 384), BF)] * 2, name="leg")


def mix_body(r_ref, k_ref, o_ref, s_ref):
    i = lax.broadcasted_iota(jnp.int32, (256, 256), 0)
    j = lax.broadcasted_iota(jnp.int32, (256, 256), 1)
    perm = ((i // 16 == j % 16) & (i % 16 == j // 16)).astype(F32).astype(BF)
    x = dot(perm, r_ref[...].reshape(256, 1536), 1, 0).astype(BF)
    for l in range(16):
        for side in range(2):
            v = x[16 * l:16 * l + 16, 768 * side:768 * side + 768]
            v = jnp.concatenate([v[:, :384], v[:, 384:]], 0)
            y = dot(v, k_ref[l], 1, side).astype(BF)
            s_ref[16 * l:16 * l + 16, 768 * side:768 * side + 384] = y[:16]
            s_ref[16 * l:16 * l + 16, 768 * side + 384:768 * side + 768] = y[16:]
    o_ref[...] = dot(perm, s_ref[...], 1, 0).astype(BF).reshape(16, 16, 1536)


def mix(r, k):
    return whole(mix_body, (16, 16, 1536), r, k, scratch=[pltpu.VMEM((256, 1536), BF)], name="mix")


def syn_body(x_ref, pf_ref, pi_ref, o_ref, y_ref, z_ref):
    for m in range(2):
        y_ref[m] = dot(pi_ref[m], x_ref[:, 384 * m:384 * m + 384], 1, 0).astype(BF)
        y_ref[2 + m] = dot(pf_ref[m], x_ref[:, 768 + 384 * m:768 + 384 * m + 384], 1, 0).astype(BF)
    for a in range(NA):
        for j in range(4):
            m, r = j // 2, j % 2
            for t in range(48):
                lane = C * r + 24 * a
                z_ref[64 + 16 * j:80 + 16 * j, 24 * t:24 * t + 24] = y_ref[m, 16 * t:16 * t + 16, lane:lane + 24]
            for k in range(SLOTS):
                row = 128 * k + 16 * a
                z_ref[16 * j:16 * j + 16, C * k:C * k + C] = y_ref[2 + m, row:row + 16, C * r:C * r + C]
        o_ref[:, a, :, :] = swap_rows(z_ref[...], 8, NP).reshape(NP, 8, W)


def syn(x, pf, pi):
    scratch = [pltpu.VMEM((4, 768, 384), BF), pltpu.VMEM((128, W), BF)]
    return whole(syn_body, (NP, NA, 8, W), x, pf, pi, scratch=scratch, name="syn").reshape(128, 8, W)


def idft_f_body(y_ref, b_ref, o_ref):
    y = y_ref[:, 4:, :].reshape(512, W)
    o_ref[...] = dot(y[:, :1080], b_ref[...], 0, 0).astype(BF)


def idft_f(y, bdt):
    return whole(idft_f_body, (1080, LON), y, bdt, name="idft_f", far=True)


def idft_g_body(y_ref, b_ref, o_hbm, o_ref, sem):
    y = y_ref[:, :4, :].reshape(512, W)
    stores = []
    for i in range(4):
        z = dot(b_ref[4 * LP * i:4 * LP * (i + 1), :], y, 1, 0).astype(BF)
        for half in range(2):
            row = 2 * LP * half
            for k in range(SLOTS):
                e = z[row:row + 90, C * k:C * k + C]
                o = z[row + LP:row + LP + 90, C * k:C * k + C]
                v = jnp.concatenate([e, o], 1)
                for t in range(3):
                    at = 272 * k + 90 * t
                    o_ref[2 * i + half, at:at + 90, :] = v[:, 128 * t:128 * t + 128]
        part = pl.ds(2 * i, 2)
        stores.append(pltpu.make_async_copy(o_ref.at[part], o_hbm.at[part], sem.at[i]))
        stores[i].start()
    for copy in stores:
        copy.wait()


def idft_g(y, bp):
    return pl.pallas_call(
        idft_g_body,
        in_specs=[VMEM, VMEM],
        out_specs=ANY,
        out_shape=pltpu.HBM((NA, WIRE, 128), BF),
        scratch_shapes=[pltpu.VMEM((NA, WIRE, 128), BF), pltpu.SemaphoreType.DMA((4,))],
        compiler_params=params(),
        name="idft_g",
    )(near(y), near(bp))


def order_tables(table, first):
    part = lax.dynamic_slice(table, (0, first, 0), (LAT, 2, DEG))
    part = part.reshape(NP, ROWS, 2, DEG).transpose(2, 1, 0, 3)
    return jnp.pad(part, ((0, 0), (0, 3), (0, 0), (0, 0))).reshape(2, 768, DEG)


def fence(*values):
    return lax.optimization_barrier(values)


def on_device(grid_input, cotangent, forward_legendre, inverse_legendre, filter_weight):
    bdt, bpt, bp = [jnp.asarray(t) for t in tables()]
    both = ("polar", "azimuth")
    first = 2 * lax.axis_index("azimuth")

    def over_all(x):
        return lax.all_to_all(x, both, 0, 0)

    def over_polar(x):
        return lax.all_to_all(x, "polar", 0, 0)

    def over_azimuth(x):
        return lax.all_to_all(x, "azimuth", 0, 0)

    spread = prep(grid_input)
    cot = cotangent.reshape(1080, LON)
    spread, cot = fence(spread, cot)
    got = over_azimuth(spread)
    wire_g = dft_g(cot, bdt)

    pf = order_tables(forward_legendre, first)
    pi = order_tables(inverse_legendre, first)
    cube = filter_weight.reshape(16, 2, C, C)
    upper = jnp.concatenate([cube[:, 0], cube[:, 1]], axis=2)
    lower = jnp.concatenate([-cube[:, 1], cube[:, 0]], axis=2)
    kernel = jnp.concatenate([upper, lower], axis=1)

    got, wire_g, pf, pi, kernel = fence(got, wire_g, pf, pi, kernel)
    modes = leg(over_all(dft_f(got, bpt, wire_g)), pf, pi)
    modes = over_polar(modes.reshape(16, 16, 1536))
    modes = over_polar(mix(modes, kernel)).reshape(DEG, 1536)
    back = over_all(syn(modes, pf, pi))
    grad = over_azimuth(idft_g(back, bp))
    filtered = idft_f(back, bdt)
    filtered, grad = fence(filtered, grad)
    return filtered.reshape(ROWS, 24, LON), post(grad)


def solution(mesh):
    return jax.shard_map(
        on_device,
        mesh=mesh,
        in_specs=(
            P("polar", "azimuth"),
            P("polar", "azimuth", None),
            P(None, "polar", None),
            P(None, "polar", None),
            P("polar", None),
        ),
        out_specs=(P("polar", "azimuth", None), P("polar", "azimuth")),
        check_vma=False,
    )
```

```python
import functools
import math
import numpy as np
import ml_dtypes
import jax
import jax.numpy as jnp
from jax import lax
from jax.sharding import PartitionSpec as P
from jax.experimental import pallas as pl
from jax.experimental.pallas import tpu as pltpu

LAT = 720
LON = 1440
C = 192
DEG = 256
ORD = 256
NP = 16
NA = 8
ROWS = 45
SLOTS = 6
PAIRS = 90
LP = 96
W = 1152
F32 = jnp.float32
BF = jnp.bfloat16


def params():
    return pltpu.CompilerParams(vmem_limit_bytes=20 << 20)


def dot(a, b, ca, cb):
    return lax.dot_general(a, b, (((ca,), (cb,)), ((), ())), preferred_element_type=F32)


def tables():
    lon = np.arange(LON)[:, None]
    m = np.arange(ORD)[None, :]
    ang = ((lon * m) % LON) * (2.0 * math.pi / LON)
    fac = 1.0 / math.sqrt(LON)
    st = np.stack([np.cos(ang) * fac, -np.sin(ang) * fac], axis=-1).astype(np.float32)
    dbl = np.where(np.arange(ORD) == 0, 1.0, 2.0).astype(np.float32)[None, :, None]
    plain = st.reshape(LON, 2 * ORD).astype(ml_dtypes.bfloat16)
    doubled = (st * dbl).reshape(LON, 2 * ORD).astype(ml_dtypes.bfloat16)
    p4 = plain.reshape(NA, PAIRS, 2, 2 * ORD).transpose(0, 2, 1, 3)
    pp = np.zeros((NA, 2, LP, 2 * ORD), ml_dtypes.bfloat16)
    pp[:, :, :PAIRS] = p4
    pp = pp.reshape(2 * NA * LP, 2 * ORD)
    return np.ascontiguousarray(doubled.T), np.ascontiguousarray(pp.T), pp


SMEM = pl.BlockSpec(memory_space=pltpu.SMEM)
VMEM = pl.BlockSpec(memory_space=pltpu.VMEM)


ANY = pl.BlockSpec(memory_space=pl.ANY)


def away(x):
    return pltpu.with_memory_space_constraint(x, pltpu.HBM)


def near(x):
    return pltpu.with_memory_space_constraint(x, pltpu.VMEM)


WIRE = 272 * SLOTS
STRIDE = 273


def slot_rows(k):
    return pl.ds(8 * k, 8 if k < 5 else 5)


def prep_body(x_hbm, o_hbm, x_ref, y_ref, s_ref, in_sem, out_sem):
    loads = []
    for k in range(SLOTS):
        rows = slot_rows(k)
        loads.append(pltpu.make_async_copy(x_hbm.at[rows, :], x_ref.at[rows, :], in_sem.at[k]))
        loads[k].start()
    stores = []
    for k in range(SLOTS):
        loads[k].wait()
        for g in range(6):
            lane, n = 5760 * g, 5760
            if k < 5:
                v = x_ref[8 * k:8 * k + 8, lane:lane + n].astype(F32)
            else:
                v = jnp.concatenate([x_ref[40:45, lane:lane + n].astype(F32), jnp.zeros((3, n), F32)], 0)
            for i in range(15):
                for t in range(3):
                    at = (3 * i + t) * 128
                    s_ref[pl.ds(90 * t + 15 * g + i, 8, stride=STRIDE), :] = v[:, at:at + 128]
        for a in range(NA):
            y_ref[a, 272 * k:272 * k + 272, :] = s_ref[STRIDE * a:STRIDE * a + 272, :].astype(BF)
        part = pl.ds(272 * k, 272)
        stores.append(pltpu.make_async_copy(y_ref.at[:, part, :], o_hbm.at[:, part, :], out_sem.at[k]))
        stores[k].start()
    for copy in stores:
        copy.wait()


def edge(body, out, x, name):
    return pl.pallas_call(
        body,
        in_specs=[ANY],
        out_specs=ANY,
        out_shape=pltpu.HBM(out, BF),
        scratch_shapes=[
            pltpu.VMEM(x.shape, BF),
            pltpu.VMEM(out, BF),
            pltpu.VMEM((STRIDE * NA, 128), F32),
            pltpu.SemaphoreType.DMA((SLOTS,)),
            pltpu.SemaphoreType.DMA((SLOTS,)),
        ],
        compiler_params=params(),
        name=name,
    )(away(x))


def prep(x):
    return edge(prep_body, (NA, WIRE, 128), x, "prep")


def post_body(r_hbm, o_hbm, r_ref, y_ref, s_ref, in_sem, out_sem):
    loads = []
    for k in range(SLOTS):
        part = pl.ds(272 * k, 272)
        loads.append(pltpu.make_async_copy(r_hbm.at[:, part, :], r_ref.at[:, part, :], in_sem.at[k]))
        loads[k].start()
    stores = []
    for k in range(SLOTS):
        loads[k].wait()
        for a in range(NA):
            s_ref[STRIDE * a:STRIDE * a + 272, :] = r_ref[a, 272 * k:272 * k + 272, :].astype(F32)
        c = 8 if k < 5 else 5
        for lp in range(PAIRS):
            for t in range(3):
                v = s_ref[pl.ds(90 * t + lp, 8, stride=STRIDE), :].astype(BF)
                at = (3 * lp + t) * 128
                y_ref[8 * k:8 * k + c, at:at + 128] = v[:c]
        rows = slot_rows(k)
        stores.append(pltpu.make_async_copy(y_ref.at[rows, :], o_hbm.at[rows, :], out_sem.at[k]))
        stores[k].start()
    for copy in stores:
        copy.wait()


def post(r):
    return edge(post_body, (ROWS, PAIRS * 384), r, "post")


def whole(body, out, *args, scratch=(), name=None, far=False):
    return pl.pallas_call(
        body,
        in_specs=[VMEM] * len(args),
        out_specs=VMEM,
        out_shape=jax.ShapeDtypeStruct(out, BF) if far else pltpu.VMEM(out, BF),
        scratch_shapes=list(scratch),
        compiler_params=params(),
        name=name,
    )(*[near(a) for a in args])


def dft_f_body(r_ref, b_hbm, g_hbm, o_ref, x_ref, w_ref, b_ref, g_ref, sem):
    load_b = pltpu.make_async_copy(b_hbm, b_ref, sem.at[0])
    load_g = pltpu.make_async_copy(g_hbm, g_ref, sem.at[1])
    load_b.start()

    def gather(to_ref, slots):
        for blk in range(NA):
            row = 2 * LP * blk
            for end in (row + LP, row + 2 * LP):
                to_ref[end - 16:end, :] = jnp.zeros((16, C * len(slots)), BF)
            for i, k in enumerate(slots):
                at = 272 * k
                v = [r_ref[blk, at + 90 * t:at + 90 * t + 90, :] for t in range(3)]
                to_ref[row:row + 90, C * i:C * i + C] = jnp.concatenate([v[0], v[1][:, :64]], 1)
                to_ref[row + LP:row + LP + 90, C * i:C * i + C] = jnp.concatenate([v[1][:, 64:], v[2]], 1)

    gather(x_ref, (0, 1, 2, 3))
    load_b.wait()
    load_g.start()
    y = dot(b_ref[...], x_ref[...], 1, 0).astype(BF)
    gather(w_ref, (4, 5))
    o_ref[:, :4, :768] = y.reshape(128, 4, 768)
    y = dot(b_ref[...], w_ref[...], 1, 0).astype(BF)
    load_g.wait()
    o_ref[:, 4:, :] = g_ref[...]
    o_ref[:, :4, 768:] = y.reshape(128, 4, 384)


def dft_f(r, bpt, wire_g):
    return pl.pallas_call(
        dft_f_body,
        in_specs=[VMEM, ANY, ANY],
        out_specs=VMEM,
        out_shape=pltpu.VMEM((128, 8, W), BF),
        scratch_shapes=[
            pltpu.VMEM((1536, 768), BF),
            pltpu.VMEM((1536, 384), BF),
            pltpu.VMEM((512, 1536), BF),
            pltpu.VMEM((128, 4, W), BF),
            pltpu.SemaphoreType.DMA((2,)),
        ],
        compiler_params=params(),
        name="dft_f",
    )(near(r), away(bpt), away(wire_g))


def dft_g_body(x_ref, b_ref, o_ref):
    y = dot(b_ref[...], x_ref[...], 1, 1).astype(BF)
    y = jnp.concatenate([y, jnp.zeros((512, W - 1080), BF)], 1)
    o_ref[...] = y.reshape(128, 4, W)


def dft_g(x, bdt):
    return whole(dft_g_body, (128, 4, W), x, bdt, name="dft_g")


def swap_rows(x, rows, cols):
    n = rows * cols
    i = lax.broadcasted_iota(jnp.int32, (n, n), 0)
    j = lax.broadcasted_iota(jnp.int32, (n, n), 1)
    perm = ((i // rows == j % cols) & (i % rows == j // cols)).astype(F32).astype(BF)
    return dot(perm, x, 1, 0).astype(BF)


def leg_body(r_ref, pf_ref, pi_ref, o_ref, v_ref, *built):
    for a in range(NA):
        v_ref[a] = swap_rows(r_ref[:, a, :, :].reshape(128, W), NP, 8)
    for m in range(2):
        s_ref, t_ref = built[2 * m], built[2 * m + 1]
        for a in range(NA):
            for r in range(2):
                j = 2 * m + r
                for k in range(SLOTS):
                    row = 128 * k + 16 * a
                    s_ref[row:row + 16, C * r:C * r + C] = v_ref[a, 16 * j:16 * j + 16, C * k:C * k + C]
                for t in range(48):
                    lane = C * r + 24 * a
                    t_ref[16 * t:16 * t + 16, lane:lane + 24] = v_ref[a, 64 + 16 * j:80 + 16 * j, 24 * t:24 * t + 24]
        o_ref[:, 384 * m:384 * m + 384] = dot(pf_ref[m], s_ref[...], 0, 0).astype(BF)
        o_ref[:, 768 + 384 * m:768 + 384 * m + 384] = dot(pi_ref[m], t_ref[...], 0, 0).astype(BF)


def leg(r, pf, pi):
    r = r.reshape(NP, NA, 8, W)
    scratch = [pltpu.VMEM((NA, 128, W), BF)] + [pltpu.VMEM((768, 384), BF)] * 4
    return whole(leg_body, (DEG, 1536), r, pf, pi, scratch=scratch, name="leg")


def mix_body(r_ref, k_ref, o_ref, s_ref):
    i = lax.broadcasted_iota(jnp.int32, (256, 256), 0)
    j = lax.broadcasted_iota(jnp.int32, (256, 256), 1)
    perm = ((i // 16 == j % 16) & (i % 16 == j // 16)).astype(F32).astype(BF)
    x = dot(perm, r_ref[...].reshape(256, 1536), 1, 0).astype(BF)
    for l in range(16):
        for side in range(2):
            v = x[16 * l:16 * l + 16, 768 * side:768 * side + 768]
            v = jnp.concatenate([v[:, :384], v[:, 384:]], 0)
            y = dot(v, k_ref[l], 1, side).astype(BF)
            s_ref[16 * l:16 * l + 16, 768 * side:768 * side + 384] = y[:16]
            s_ref[16 * l:16 * l + 16, 768 * side + 384:768 * side + 768] = y[16:]
    o_ref[...] = dot(perm, s_ref[...], 1, 0).astype(BF).reshape(16, 16, 1536)


def mix(r, k):
    return whole(mix_body, (16, 16, 1536), r, k, scratch=[pltpu.VMEM((256, 1536), BF)], name="mix")


def syn_body(x_ref, pf_ref, pi_ref, o_ref, z_ref, *parts):
    for m in range(2):
        f_ref, g_ref = parts[2 * m], parts[2 * m + 1]
        f_ref[...] = dot(pi_ref[m], x_ref[:, 384 * m:384 * m + 384], 1, 0).astype(BF)
        g_ref[...] = dot(pf_ref[m], x_ref[:, 768 + 384 * m:768 + 384 * m + 384], 1, 0).astype(BF)
        for a in range(NA):
            for r in range(2):
                j = 2 * m + r
                for t in range(48):
                    lane = C * r + 24 * a
                    z_ref[a, 64 + 16 * j:80 + 16 * j, 24 * t:24 * t + 24] = f_ref[16 * t:16 * t + 16, lane:lane + 24]
                for k in range(SLOTS):
                    row = 128 * k + 16 * a
                    z_ref[a, 16 * j:16 * j + 16, C * k:C * k + C] = g_ref[row:row + 16, C * r:C * r + C]
    for a in range(NA):
        o_ref[:, a, :, :] = swap_rows(z_ref[a], 8, NP).reshape(NP, 8, W)


def syn(x, pf, pi):
    scratch = [pltpu.VMEM((NA, 128, W), BF)] + [pltpu.VMEM((768, 384), BF)] * 4
    return whole(syn_body, (NP, NA, 8, W), x, pf, pi, scratch=scratch, name="syn").reshape(128, 8, W)


def idft_f_body(y_ref, b_ref, o_ref):
    y = y_ref[:, 4:, :].reshape(512, W)
    o_ref[...] = dot(y[:, :1080], b_ref[...], 0, 0).astype(BF)


def idft_f(y, bdt):
    return whole(idft_f_body, (1080, LON), y, bdt, name="idft_f", far=True)


def idft_g_body(y_ref, b_ref, o_hbm, o_ref, sem):
    y = y_ref[:, :4, :].reshape(512, W)
    stores = []
    for blk in range(NA):
        z = dot(b_ref[2 * LP * blk:2 * LP * (blk + 1), :], y, 1, 0).astype(BF)
        for k in range(SLOTS):
            e = z[:90, C * k:C * k + C]
            o = z[LP:LP + 90, C * k:C * k + C]
            v = jnp.concatenate([e, o], 1)
            for t in range(3):
                at = 272 * k + 90 * t
                o_ref[blk, at:at + 90, :] = v[:, 128 * t:128 * t + 128]
        stores.append(pltpu.make_async_copy(o_ref.at[blk], o_hbm.at[blk], sem.at[blk]))
        stores[blk].start()
    for copy in stores:
        copy.wait()


def idft_g(y, bp):
    return pl.pallas_call(
        idft_g_body,
        in_specs=[VMEM, VMEM],
        out_specs=ANY,
        out_shape=pltpu.HBM((NA, WIRE, 128), BF),
        scratch_shapes=[pltpu.VMEM((NA, WIRE, 128), BF), pltpu.SemaphoreType.DMA((NA,))],
        compiler_params=params(),
        name="idft_g",
    )(near(y), near(bp))


def order_tables(table, first):
    part = lax.dynamic_slice(table, (0, first, 0), (LAT, 2, DEG))
    part = part.reshape(NP, ROWS, 2, DEG).transpose(2, 1, 0, 3)
    return jnp.pad(part, ((0, 0), (0, 3), (0, 0), (0, 0))).reshape(2, 768, DEG)


def fence(*values):
    return lax.optimization_barrier(values)


def on_device(grid_input, cotangent, forward_legendre, inverse_legendre, filter_weight):
    bdt, bpt, bp = [jnp.asarray(t) for t in tables()]
    both = ("polar", "azimuth")
    first = 2 * lax.axis_index("azimuth")

    def over_all(x):
        return lax.all_to_all(x, both, 0, 0)

    def over_polar(x):
        return lax.all_to_all(x, "polar", 0, 0)

    def over_azimuth(x):
        return lax.all_to_all(x, "azimuth", 0, 0)

    spread = prep(grid_input)
    cot = cotangent.reshape(1080, LON)
    spread, cot = fence(spread, cot)
    got = over_azimuth(spread)
    wire_g = dft_g(cot, bdt)

    pf = order_tables(forward_legendre, first)
    pi = order_tables(inverse_legendre, first)
    cube = filter_weight.reshape(16, 2, C, C)
    upper = jnp.concatenate([cube[:, 0], cube[:, 1]], axis=2)
    lower = jnp.concatenate([-cube[:, 1], cube[:, 0]], axis=2)
    kernel = jnp.concatenate([upper, lower], axis=1)

    got, wire_g, pf, pi, kernel = fence(got, wire_g, pf, pi, kernel)
    modes = leg(over_all(dft_f(got, bpt, wire_g)), pf, pi)
    modes = over_polar(modes.reshape(16, 16, 1536))
    modes = over_polar(mix(modes, kernel)).reshape(DEG, 1536)
    back = over_all(syn(modes, pf, pi))
    grad = over_azimuth(idft_g(back, bp))
    filtered = idft_f(back, bdt)
    filtered, grad = fence(filtered, grad)
    return filtered.reshape(ROWS, 24, LON), post(grad)


def solution(mesh):
    return jax.shard_map(
        on_device,
        mesh=mesh,
        in_specs=(
            P("polar", "azimuth"),
            P("polar", "azimuth", None),
            P(None, "polar", None),
            P(None, "polar", None),
            P("polar", None),
        ),
        out_specs=(P("polar", "azimuth", None), P("polar", "azimuth")),
        check_vma=False,
    )
```
